256 devices in a mesh: dp: 16 (over y, x_lo, core), cells: 16 (over z, x_hi).
Axes of the slice: x: 4 (x_hi: 2, x_lo: 2; x = x_hi * 2 + x_lo), y: 4, z: 8, core: 2. Of those that a mesh axis runs over, the one named last changes fastest.
Arguments:
- source_field: bfloat16 [48, 8, 12288], P(None, None, 'cells'), may hold values from -85 to 85, as said below
- receiver_field: bfloat16 [512, 8, 12288], P('dp', None, 'cells'), may hold values from -6 to 6
- source_index: int32 [8192], P('dp'), may hold values from 0 to 47
- receiver_index: int32 [8192], P('dp'), may hold values from 0 to 511, as said below
- observed: float32 [8192], P('dp'), may hold values from -6 to 6
- noise_code: int32 [8, 8192], P(None, 'dp'), may hold values from -4096 to 4096
- huber_code: int32 [8], replicated, may hold values from 8 to 40
- start_model: float32 [12288], P('cells'), may hold values from -6 to 6
Outputs:
- models: float32 [8, 12288], P(None, 'cells')
The draws below stay inside these ranges and needn't reach their ends.
Inputs may be any that keep to these rules, and one draw needn't show every extreme that they name: `source_field`: entries of order one to ten; the scale varies from cell to cell. `receiver_index`: in each aligned block of 512 data, exactly 512 // 16 data name a receiver in each range [j * 32, (j + 1) * 32).
All inputs are finite; a program needn't handle non-finite values.
Results may differ from the reference program's by a relative error of at most 0.0011.
Values may be sent and summed in bfloat16 or wider, within the bound.
A program may use at most 64 MiB of HBM per device.

```python
import math
import jax
import jax.numpy as jnp
from jax import lax

D_DEV = 512
REC_DEV = 32
NS = 48
COMP = 8
REAL = 8
ITERS = 2
ND = 8192
NCELL = 12288
NREC = 512


def draw_source_field(key, part):
    first, second = jax.random.split(key, 2)
    values = jnp.clip(jax.random.normal(first, (NS, COMP, NCELL), jnp.float32), -6.0, 6.0)
    cell_scale = jnp.exp(jax.random.uniform(second, (1, 1, NCELL), jnp.float32, 0.0, math.log(10.0)))
    return (values * cell_scale).astype(jnp.bfloat16)


def draw_receiver_index(key, part):
    first, second = jax.random.split(jax.random.fold_in(key, 7171))
    owners = NREC // REC_DEV
    blocks = ND // D_DEV
    per_owner = D_DEV // owners
    base = (jnp.arange(D_DEV, dtype=jnp.int32) // per_owner).astype(jnp.int32)
    keys = jax.random.split(first, blocks)
    owner_rows = jax.vmap(lambda k: jax.random.permutation(k, base))(keys).reshape(ND)
    local = jax.random.randint(second, (ND,), 0, REC_DEV, jnp.int32)
    return (owner_rows * REC_DEV + local).astype(jnp.int32)


def plant(drawn, rng, low, largest):
    spot = [jax.random.randint(jax.random.fold_in(rng, axis), (), 0, length) for axis, length in enumerate(drawn.shape)]
    main_axis = drawn.shape.index(max(drawn.shape))
    beside = spot[:main_axis] + [(spot[main_axis] + 1) % drawn.shape[main_axis]] + spot[main_axis + 1:]
    return drawn.at[tuple(spot)].set(low).at[tuple(beside)].set(largest)


def levels(own_key, dims, cuts, smallest, top_value):
    def one(axis_at, blocks):
        heights = jax.random.uniform(jax.random.fold_in(jax.random.fold_in(own_key, 6), axis_at), (blocks,), jnp.float32, smallest / len(cuts), top_value / len(cuts))
        return jnp.repeat(jnp.exp(heights), dims[axis_at] // blocks).reshape((-1,) + (1,) * (len(dims) - axis_at - 1))

    factor_of = one(*cuts[0])
    for cut in cuts[1:]:
        factor_of = factor_of * one(*cut)
    return factor_of


def normal_values(stream_key, extent, spread, limit, cuts=(), kind=jnp.bfloat16):
    drawn = jax.random.normal(stream_key, extent, jnp.float32) * spread
    if len(cuts) > 0:
        drawn = levels(stream_key, extent, cuts, -0.22, 0.18) * drawn
    return jnp.clip(drawn, min=-limit, max=limit).astype(kind)


def setup_inputs(seed: int = 0) -> dict:
    key_of = jax.random.split(jax.random.key(seed), 9)
    source_field = draw_source_field(jax.random.fold_in(key_of[8], 71), 0)
    receiver_field = normal_values(key_of[1], (NREC, COMP, NCELL), 1.0, 6.0, ((0, 16), (2, 16)))
    source_index = plant(jax.random.randint(key_of[2], (ND,), 0, NS), jax.random.fold_in(key_of[2], 1), 0, NS - 1).astype(jnp.int32)
    receiver_index = draw_receiver_index(jax.random.fold_in(key_of[8], 71), 0)
    observed = normal_values(key_of[4], (ND,), 1.0, 6.0, ((0, 16),), jnp.float32)
    noise_code = plant(jax.random.randint(key_of[5], (REAL, ND), -4096, 4097), jax.random.fold_in(key_of[5], 1), -4096, 4096).astype(jnp.int32)
    huber_code = plant(jax.random.randint(key_of[6], (REAL,), 8, 41), jax.random.fold_in(key_of[6], 1), 8, 40).astype(jnp.int32)
    start_model = normal_values(key_of[7], (NCELL,), 1.0, 6.0, ((0, 16),), jnp.float32)
    return dict(source_field=source_field, receiver_field=receiver_field, source_index=source_index, receiver_index=receiver_index, observed=observed, noise_code=noise_code, huber_code=huber_code, start_model=start_model)


def form_kernel(source_field, receiver_field, source_rows, receiver_rows):
    total = jnp.zeros((source_rows.shape[0], source_field.shape[2]), jnp.float32)
    for component in range(source_field.shape[1]):
        factor = 1.0 if component % 2 == 0 else -1.0
        source_part = source_field[source_rows, component, :].astype(jnp.float32)
        receiver_part = receiver_field[receiver_rows, component, :].astype(jnp.float32)
        total = total + factor * (source_part * receiver_part)
    return (total * (0.2 / math.sqrt(COMP * NCELL))).astype(jnp.bfloat16)

def reference(source_field, receiver_field, source_index, receiver_index, observed, noise_code, huber_code, start_model):
    count = huber_code.shape[0]
    thresh = (huber_code.astype(jnp.float32) / 16.0)[:, None]
    shifted = observed[None, :] + noise_code.astype(jnp.float32) / 4096.0
    blocks = source_index.shape[0] // D_DEV
    source_blocks = source_index.reshape(blocks, D_DEV)
    receiver_blocks = receiver_index.reshape(blocks, D_DEV)
    shift_blocks = shifted.reshape(count, blocks, D_DEV).transpose(1, 0, 2)
    models = jnp.broadcast_to(start_model[None, :], (count, start_model.shape[0])).astype(jnp.float32)
    velocity = jnp.zeros_like(models)
    for iteration in range(ITERS):
        model_half = models.astype(jnp.bfloat16)

        def visit(gradient, block):
            source_rows, receiver_rows, shift_rows = block
            kernel = form_kernel(source_field, receiver_field, source_rows, receiver_rows)
            predicted = lax.dot_general(model_half, kernel, (((1,), (1,)), ((), ())), preferred_element_type=jnp.float32)
            weighted = jnp.clip(predicted - shift_rows, -thresh, thresh).astype(jnp.bfloat16)
            return (gradient + jnp.dot(weighted, kernel, preferred_element_type=jnp.float32), None)
        gradient, unused = lax.scan(visit, jnp.zeros_like(models), (source_blocks, receiver_blocks, shift_blocks))
        scale_now = jnp.sqrt(lax.optimization_barrier(jnp.mean(gradient * gradient, axis=1, keepdims=True)) + 1e-06)
        velocity = 0.9 * velocity + gradient / scale_now
        models = models - 0.1 * velocity
    return models
```

```python
import functools
import math

import jax
import jax.numpy as jnp
from jax import lax
from jax.experimental import pallas as pl
from jax.experimental.pallas import tpu as pltpu
from jax.sharding import PartitionSpec as P

F32 = jnp.float32
BF16 = jnp.bfloat16
GROUP = 16
COMP = 8
REAL = 8
MESH = pl.DeviceIdType.MESH


def iota(shape, axis):
    return lax.broadcasted_iota(jnp.int32, shape, axis)


def dot(a, b):
    return jnp.dot(a, b, preferred_element_type=F32)


def dot_nt(a, b):
    return lax.dot_general(a, b, (((1,), (1,)), ((), ())), preferred_element_type=F32)


def split_halves(table):
    high = table.astype(BF16).astype(F32)
    return jnp.where(iota(table.shape, 1) < 64, high, table - high).astype(BF16)


def body(
    cells_total,
    src_ref,
    rec_ref,
    sidx_ref,
    ridx_ref,
    obs_ref,
    noise_ref,
    huber_ref,
    start_ref,
    out_ref,
    sc,
    rc,
    data_s,
    data_r,
    tab_s,
    tab_r,
    g1_s,
    g1_r,
    g1_a,
    dl_s,
    dl_r,
    q1_s,
    q1_r,
    g2_s,
    g2_r,
    g2_a,
    q2_s,
    q2_r,
    send_sem,
    recv_sem,
):
    me_dp = lax.axis_index("dp")
    me_cells = lax.axis_index("cells")
    cells = start_ref.shape[1]
    n_data = sidx_ref.shape[1]
    scale = 0.2 / math.sqrt(COMP * cells_total)

    def peer(axis, offset):
        me = me_dp if axis == "dp" else me_cells
        return lax.rem(me + offset, GROUP)

    barrier = pltpu.get_barrier_semaphore()

    def greet(offset, carry):
        for axis in ("dp", "cells"):
            pl.semaphore_signal(
                barrier, inc=1, device_id={axis: peer(axis, offset)}, device_id_type=MESH
            )
        return carry

    lax.fori_loop(1, GROUP, greet, 0)

    def send_all(axis, phase, src_of, dst_of):
        def one(offset, carry):
            other = peer(axis, offset)
            pltpu.make_async_remote_copy(
                src_ref=src_of(other),
                dst_ref=dst_of(offset),
                send_sem=send_sem.at[phase],
                recv_sem=recv_sem.at[phase],
                device_id={axis: other},
                device_id_type=MESH,
            ).start()
            return carry

        lax.fori_loop(1, GROUP, one, 0)

    def wait_all(sem, phase, ref):
        part = ref.at[pl.ds(0, GROUP - 1)]
        pltpu.make_async_copy(part, part, sem.at[phase]).wait()

    pick = (
        (iota((128, 128), 0) % 16) * COMP + iota((128, 128), 0) // 16 == iota((128, 128), 1)
    ).astype(F32).astype(BF16)
    zero_rows = jnp.zeros((16, cells), BF16)
    for chunk in range(3):
        rows = dot(pick, src_ref[128 * chunk : 128 * chunk + 128, :]).astype(BF16)
        for c in range(COMP):
            part = rows[16 * c : 16 * c + 16, :]
            sc[c, 16 * chunk : 16 * chunk + 16, :] = part
            sc[c, 64 + 16 * chunk : 80 + 16 * chunk, :] = part
    for c in range(COMP):
        sc[c, 48:64, :] = zero_rows
        sc[c, 112:128, :] = zero_rows
    for chunk in range(2):
        rows = dot(pick, rec_ref[128 * chunk : 128 * chunk + 128, :])
        for c in range(COMP):
            part = rows[16 * c : 16 * c + 16, :]
            rc[c, 16 * chunk : 16 * chunk + 16, :] = part if c % 2 == 0 else -part

    start = start_ref[...]
    start_half = start.astype(BF16).astype(F32)
    table = jnp.zeros((64, 128), F32)
    for c in range(COMP):
        exact = rc[c] * start_half
        high = exact.astype(BF16)
        low = (exact - high.astype(F32)).astype(BF16)
        table = table + dot_nt(jnp.concatenate([high, low], axis=0), sc[c])
    table = (table[0:32] + table[32:64]) * scale
    left = iota((8, 128), 1) < 64
    tab_s[0] = jnp.where(left, table[0:8], table[8:16])
    tab_s[1] = jnp.where(left, table[16:24], table[24:32])

    pl.semaphore_wait(barrier, 2 * (GROUP - 1))
    send_all("cells", 1, lambda o: tab_s, lambda off: tab_r.at[off - 1])

    owner = ridx_ref[...] // 32
    local = ridx_ref[...] % 32
    member = (iota((16, n_data), 0) == owner).astype(F32)
    before = (iota((n_data, n_data), 0) < iota((n_data, n_data), 1)).astype(F32).astype(BF16)
    rank = jnp.sum(member * dot(member.astype(BF16), before), axis=0, keepdims=True)
    place = (128 * (owner // 4) + 32 * ((owner + me_dp) % 4)).astype(F32) + rank
    move = (iota((n_data, n_data), 0).astype(F32) == place).astype(F32).astype(BF16)
    shifted = obs_ref[...] + noise_ref[...].astype(F32) / 4096.0
    high = shifted.astype(BF16).astype(F32)
    middle = (shifted - high).astype(BF16).astype(F32)
    low = shifted - high - middle
    row8 = iota((8, n_data), 0)
    index_rows = jnp.where(
        row8 == 0,
        sidx_ref[...].astype(F32),
        jnp.where(row8 == 1, local.astype(F32), 0.0),
    )
    moved = dot_nt(jnp.concatenate([high, middle, low, index_rows], axis=0).astype(BF16), move)
    shifted = moved[0:8] + moved[8:16] + moved[16:24]
    for t in range(4):
        data_s[t, 0:8, :] = shifted[:, 128 * t : 128 * t + 128]
        data_s[t, 8:16, :] = moved[24:32, 128 * t : 128 * t + 128]
    send_all("dp", 0, lambda o: data_s.at[o // 4], lambda off: data_r.at[off - 1])
    data_r[GROUP - 1] = data_s[me_dp // 4]
    wait_all(recv_sem, 0, data_r)
    quarter = iota((16, 128), 1) // 32
    tiles = []
    for t in range(4):
        tile = data_r[4 * t]
        for o in range(4 * t + 2, 4 * t + 5):
            here = lax.rem(2 * me_dp + 32 - o, 4)
            tile = jnp.where(quarter == here, data_r[o - 1], tile)
        tiles.append(tile)
    data = jnp.concatenate(tiles, axis=1)
    shifted = data[0:8]
    source = data[8:9].astype(jnp.int32)
    receiver = data[9:10].astype(jnp.int32)
    is_source = (iota((128, n_data), 0) % 64 == source).astype(F32).astype(BF16)
    is_receiver = (iota((32, n_data), 0) == receiver).astype(F32)
    limit = jnp.zeros((REAL, n_data), F32)
    for k in range(REAL):
        limit = jnp.where(row8 == k, huber_ref[k].astype(F32) / 16.0, limit)

    wait_all(recv_sem, 1, tab_r)
    packed = tab_s[...]
    for o in range(GROUP - 1):
        packed = packed + tab_r[o]
    rows = []
    for t in range(2):
        here = packed[t]
        turned = pltpu.roll(here, 64, 1)
        rows.append(jnp.where(left, here, turned))
        rows.append(jnp.where(left, turned, here))
    spread = dot(split_halves(jnp.concatenate(rows, axis=0)), is_source)
    predicted = jnp.sum(spread * is_receiver, axis=0, keepdims=True)

    def gradient(predicted, out):
        weighted = jnp.clip(predicted - shifted, -limit, limit).astype(BF16).astype(F32)
        spread = [(weighted[k : k + 1, :] * is_receiver).astype(BF16) for k in range(REAL)]
        pairs = split_halves(dot_nt(jnp.concatenate(spread, axis=0), is_source))
        for b in range(cells // 256):
            lanes = slice(256 * b, 256 * b + 256)
            total = [jnp.zeros((8, 256), F32) for k in range(REAL)]
            for c in range(COMP):
                mixed = dot(pairs, sc[c, :, lanes])
                field = rc[c, :, lanes]
                for k in range(REAL):
                    product = mixed[32 * k : 32 * k + 32] * field
                    total[k] = total[k] + (
                        (product[0:8] + product[8:16]) + (product[16:24] + product[24:32])
                    )
            for k in range(REAL):
                row = jnp.sum(total[k], axis=0, keepdims=True) * scale
                for half in range(2):
                    t = 2 * b + half
                    at = 128 * (t % 3)
                    out[2 * k + t // 3, :, at : at + 128] = row[:, 128 * half : 128 * half + 128]

    def reduce_gradient(phase, part, arrived, whole):
        send_all("dp", phase, lambda o: part.at[o], lambda off: arrived.at[off - 1])
        mine = part[me_dp]
        wait_all(recv_sem, phase, arrived)
        for o in range(GROUP - 1):
            mine = mine + arrived[o]
        whole[me_dp] = mine
        send_all("dp", phase + 1, lambda o: whole.at[me_dp], lambda off: whole.at[me_dp])
        wait_all(recv_sem, phase + 1, whole)
        return [
            jnp.concatenate([whole[2 * k], whole[2 * k + 1]], axis=1) for k in range(REAL)
        ]

    def square_sums(rows):
        total = jnp.zeros((1, 128), F32)
        for k in range(REAL):
            one = jnp.sum(rows[k] * rows[k], axis=1, keepdims=True)
            total = jnp.where(iota((1, 128), 1) == k, one, total)
        return total

    def inverse_scale(own, arrived):
        total = own
        for o in range(GROUP - 1):
            total = total + arrived[o]
        diagonal = iota((8, 128), 0) == iota((8, 128), 1)
        column = jnp.sum(jnp.where(diagonal, total, 0.0), axis=1, keepdims=True)
        return 1.0 / jnp.sqrt(column / cells_total + 1e-06)

    gradient(predicted, g1_s)
    first = reduce_gradient(2, g1_s, g1_r, g1_a)

    table = jnp.zeros((32 * REAL, 128), F32)
    for c in range(COMP):
        field = rc[c]
        scaled = [(field * first[k]).astype(BF16) for k in range(REAL)]
        table = table + dot_nt(jnp.concatenate(scaled, axis=0), sc[c])
    spread = dot(split_halves(table * scale), is_source)
    change = jnp.concatenate(
        [
            jnp.sum(spread[32 * k : 32 * k + 32] * is_receiver, axis=0, keepdims=True)
            for k in range(REAL)
        ],
        axis=0,
    )
    half = n_data // 2
    dl_s[...] = jnp.concatenate([change[:, :half], change[:, half:]], axis=0).astype(BF16)
    q1_s[...] = square_sums(first)
    send_all("cells", 4, lambda o: dl_s, lambda off: dl_r.at[off - 1])
    send_all("cells", 5, lambda o: q1_s, lambda off: q1_r.at[off - 1])
    wait_all(recv_sem, 5, q1_r)
    inverse1 = inverse_scale(q1_s[...], q1_r)
    wait_all(recv_sem, 4, dl_r)
    total = dl_s[...].astype(F32)
    for o in range(GROUP - 1):
        total = total + dl_r[o].astype(F32)
    change = jnp.concatenate([total[0:8], total[8:16]], axis=1)
    gradient(predicted - 0.1 * (change * inverse1), g2_s)
    second = reduce_gradient(6, g2_s, g2_r, g2_a)
    q2_s[...] = square_sums(second)
    send_all("cells", 8, lambda o: q2_s, lambda off: q2_r.at[off - 1])
    velocity = jnp.concatenate(first, axis=0) * inverse1
    base = (start - 0.1 * velocity) - 0.1 * (0.9 * velocity)
    step = jnp.concatenate(second, axis=0)
    wait_all(recv_sem, 8, q2_r)
    out_ref[...] = base - 0.1 * (step * inverse_scale(q2_s[...], q2_r))

    for phase, ref in enumerate((data_r, tab_r, g1_r, g1_a, dl_r, q1_r, g2_r, g2_a, q2_r)):
        wait_all(send_sem, phase, ref)


def on_device(source, receiver, source_index, receiver_index, observed, noise, huber, start):
    cells = start.shape[0]
    n_data = source_index.shape[0]
    near = GROUP - 1
    vmem = pl.BlockSpec(memory_space=pltpu.VMEM)
    row = pltpu.VMEM((1, 128), F32)
    rows = pltpu.VMEM((near, 1, 128), F32)
    chunk = REAL * cells // GROUP
    return pl.pallas_call(
        functools.partial(body, cells * GROUP),
        out_shape=jax.ShapeDtypeStruct((REAL, cells), F32),
        in_specs=[vmem] * 6 + [pl.BlockSpec(memory_space=pltpu.SMEM), vmem],
        out_specs=vmem,
        scratch_shapes=[
            pltpu.VMEM((COMP, 128, cells), BF16),
            pltpu.VMEM((COMP, 32, cells), F32),
            pltpu.VMEM((4, 16, 128), F32),
            pltpu.VMEM((GROUP, 16, 128), F32),
            pltpu.VMEM((2, 8, 128), F32),
            pltpu.VMEM((near, 2, 8, 128), F32),
            pltpu.VMEM((GROUP, 1, chunk), F32),
            pltpu.VMEM((near, 1, chunk), F32),
            pltpu.VMEM((GROUP, 1, chunk), F32),
            pltpu.VMEM((16, n_data // 2), BF16),
            pltpu.VMEM((near, 16, n_data // 2), BF16),
            row,
            rows,
            pltpu.VMEM((GROUP, 1, chunk), F32),
            pltpu.VMEM((near, 1, chunk), F32),
            pltpu.VMEM((GROUP, 1, chunk), F32),
            row,
            rows,
            pltpu.SemaphoreType.DMA((9,)),
            pltpu.SemaphoreType.DMA((9,)),
        ],
        compiler_params=pltpu.CompilerParams(collective_id=0, has_side_effects=True),
    )(
        source.reshape(-1, cells),
        receiver.reshape(-1, cells),
        source_index.reshape(1, n_data),
        receiver_index.reshape(1, n_data),
        observed.reshape(1, n_data),
        noise,
        huber,
        start.reshape(1, cells),
    )


def solution(mesh):
    placed = (
        P(None, None, "cells"),
        P("dp", None, "cells"),
        P("dp"),
        P("dp"),
        P("dp"),
        P(None, "dp"),
        P(),
        P("cells"),
    )
    return jax.shard_map(
        on_device, mesh=mesh, in_specs=placed, out_specs=P(None, "cells"), check_vma=False
    )
```

```python
import functools
import math

import jax
import jax.numpy as jnp
from jax import lax
from jax.experimental import pallas as pl
from jax.experimental.pallas import tpu as pltpu
from jax.sharding import PartitionSpec as P

F32 = jnp.float32
BF16 = jnp.bfloat16
GROUP = 16
COMP = 8
REAL = 8
MESH = pl.DeviceIdType.MESH
FAR_FIRST = sorted(range(1, GROUP), key=lambda o: -min(o, GROUP - o))


def iota(shape, axis):
    return lax.broadcasted_iota(jnp.int32, shape, axis)


def dot(a, b):
    return jnp.dot(a, b, preferred_element_type=F32)


def dot_nt(a, b):
    return lax.dot_general(a, b, (((1,), (1,)), ((), ())), preferred_element_type=F32)


def split_halves(table):
    high = table.astype(BF16).astype(F32)
    return jnp.where(iota(table.shape, 1) < 64, high, table - high).astype(BF16)


def body(
    cells_total,
    *refs,
):
    given, out_ref, held, refs = refs[:8], refs[8], refs[9:17], refs[17:]
    src_ref, rec_ref, sidx_ref, ridx_ref, obs_ref, noise_ref, huber_ref, start_ref = held
    sc, rc, grad, data_s, data_r, tab_s, tab_r, g1_s, g1_r, dl_s, dl_r, q1_s, q1_r = refs[:13]
    g2_s, g2_r, q2_s, q2_r, send_sem, recv_sem, load_sem = refs[13:]
    me_dp = lax.axis_index("dp")
    me_cells = lax.axis_index("cells")
    cells = src_ref.shape[1]
    n_data = sidx_ref.shape[1]
    scale = 0.2 / math.sqrt(COMP * cells_total)

    def peer(axis, offset):
        me = me_dp if axis == "dp" else me_cells
        return lax.rem(me + offset, GROUP)

    barrier = pltpu.get_barrier_semaphore()

    for offset in FAR_FIRST:
        for axis in ("cells", "dp"):
            pl.semaphore_signal(
                barrier, inc=1, device_id={axis: peer(axis, offset)}, device_id_type=MESH
            )
    loads = [
        pltpu.make_async_copy(a, b, load_sem.at[n]) for n, (a, b) in enumerate(zip(given, held))
    ]
    for n in (1, 7, 0, 2, 3, 4, 5, 6):
        loads[n].start()

    def send_all(axis, phase, src_of, dst_of):
        for offset in FAR_FIRST:
            other = peer(axis, offset)
            pltpu.make_async_remote_copy(
                src_ref=src_of(other),
                dst_ref=dst_of(offset),
                send_sem=send_sem.at[phase],
                recv_sem=recv_sem.at[phase],
                device_id={axis: other},
                device_id_type=MESH,
            ).start()

    def wait_all(sem, phase, ref):
        part = ref.at[pl.ds(0, GROUP - 1)]
        pltpu.make_async_copy(part, part, sem.at[phase]).wait()

    pick = (
        (iota((128, 128), 0) % 16) * COMP + iota((128, 128), 0) // 16 == iota((128, 128), 1)
    ).astype(F32).astype(BF16)
    loads[1].wait()
    for chunk in range(2):
        rows = dot(pick, rec_ref[128 * chunk : 128 * chunk + 128, :])
        for c in range(COMP):
            part = rows[16 * c : 16 * c + 16, :]
            rc[c, 16 * chunk : 16 * chunk + 16, :] = part if c % 2 == 0 else -part
    loads[0].wait()
    zero_rows = jnp.zeros((16, cells), BF16)
    for chunk in range(3):
        rows = dot(pick, src_ref[128 * chunk : 128 * chunk + 128, :]).astype(BF16)
        for c in range(COMP):
            part = rows[16 * c : 16 * c + 16, :]
            sc[c, 16 * chunk : 16 * chunk + 16, :] = part
            sc[c, 64 + 16 * chunk : 80 + 16 * chunk, :] = part
    for c in range(COMP):
        sc[c, 48:64, :] = zero_rows
        sc[c, 112:128, :] = zero_rows

    loads[7].wait()
    start = jnp.concatenate([start_ref[n : n + 1, :] for n in range(cells // 128)], axis=1)
    start_half = start.astype(BF16).astype(F32)
    table = jnp.zeros((64, 128), F32)
    for c in range(COMP):
        exact = rc[c] * start_half
        high = exact.astype(BF16)
        low = (exact - high.astype(F32)).astype(BF16)
        table = table + dot_nt(jnp.concatenate([high, low], axis=0), sc[c])
    table = (table[0:32] + table[32:64]) * scale
    left = iota((8, 128), 1) < 64
    tab_s[0] = jnp.where(left, table[0:8], table[8:16])
    tab_s[1] = jnp.where(left, table[16:24], table[24:32])

    pl.semaphore_wait(barrier, 2 * (GROUP - 1))
    send_all("cells", 1, lambda o: tab_s, lambda off: tab_r.at[off - 1])

    for n in range(2, 7):
        loads[n].wait()
    owner = ridx_ref[...] // 32
    local = ridx_ref[...] % 32
    member = (iota((16, n_data), 0) == owner).astype(F32)
    before = (iota((n_data, n_data), 0) < iota((n_data, n_data), 1)).astype(F32).astype(BF16)
    rank = jnp.sum(member * dot(member.astype(BF16), before), axis=0, keepdims=True)
    place = (128 * (owner // 4) + 32 * ((owner + me_dp) % 4)).astype(F32) + rank
    move = (iota((n_data, n_data), 0).astype(F32) == place).astype(F32).astype(BF16)
    shifted = obs_ref[...] + noise_ref[...].astype(F32) / 4096.0
    high = shifted.astype(BF16).astype(F32)
    middle = (shifted - high).astype(BF16).astype(F32)
    low = shifted - high - middle
    row8 = iota((8, n_data), 0)
    index_rows = jnp.where(
        row8 == 0,
        sidx_ref[...].astype(F32),
        jnp.where(row8 == 1, local.astype(F32), 0.0),
    )
    moved = dot_nt(jnp.concatenate([high, middle, low, index_rows], axis=0).astype(BF16), move)
    shifted = moved[0:8] + moved[8:16] + moved[16:24]
    for t in range(4):
        data_s[t, 0:8, :] = shifted[:, 128 * t : 128 * t + 128]
        data_s[t, 8:16, :] = moved[24:32, 128 * t : 128 * t + 128]
    send_all("dp", 0, lambda o: data_s.at[o // 4], lambda off: data_r.at[off - 1])
    data_r[GROUP - 1] = data_s[me_dp // 4]
    wait_all(recv_sem, 0, data_r)
    quarter = iota((16, 128), 1) // 32
    tiles = []
    for t in range(4):
        tile = data_r[4 * t]
        for o in range(4 * t + 2, 4 * t + 5):
            here = lax.rem(2 * me_dp + 32 - o, 4)
            tile = jnp.where(quarter == here, data_r[o - 1], tile)
        tiles.append(tile)
    data = jnp.concatenate(tiles, axis=1)
    shifted = data[0:8]
    source = data[8:9].astype(jnp.int32)
    receiver = data[9:10].astype(jnp.int32)
    is_source = (iota((128, n_data), 0) % 64 == source).astype(F32).astype(BF16)
    is_receiver = (iota((32, n_data), 0) == receiver).astype(F32)
    limit = jnp.zeros((REAL, n_data), F32)
    for k in range(REAL):
        limit = jnp.where(row8 == k, huber_ref[k].astype(F32) / 16.0, limit)

    wait_all(recv_sem, 1, tab_r)
    packed = tab_s[...]
    for o in range(GROUP - 1):
        packed = packed + tab_r[o]
    rows = []
    for t in range(2):
        here = packed[t]
        turned = pltpu.roll(here, 64, 1)
        rows.append(jnp.where(left, here, turned))
        rows.append(jnp.where(left, turned, here))
    spread = dot(split_halves(jnp.concatenate(rows, axis=0)), is_source)
    predicted = jnp.sum(spread * is_receiver, axis=0, keepdims=True)

    def fold(x):
        half = x.shape[1] // 2
        return jnp.concatenate([x[:, :half], x[:, half:]], axis=0)

    def unfold(x):
        half = x.shape[0] // 2
        return jnp.concatenate([x[:half], x[half:]], axis=1)

    def sum_slots(arrived):
        parts = [arrived[o].astype(F32) for o in range(GROUP)]
        while len(parts) > 1:
            parts = [a + b for a, b in zip(parts[::2], parts[1::2])]
        return parts[0]

    def gradient(predicted, out):
        weighted = jnp.clip(predicted - shifted, -limit, limit).astype(BF16).astype(F32)
        spread = [(weighted[k : k + 1, :] * is_receiver).astype(BF16) for k in range(REAL)]
        pairs = split_halves(dot_nt(jnp.concatenate(spread, axis=0), is_source))
        for b in range(cells // 256):
            lanes = slice(256 * b, 256 * b + 256)
            total = [jnp.zeros((8, 256), F32) for k in range(REAL)]
            for c in range(COMP):
                mixed = dot(pairs, sc[c, :, lanes])
                field = rc[c, :, lanes]
                for k in range(REAL):
                    product = mixed[32 * k : 32 * k + 32] * field
                    total[k] = total[k] + (
                        (product[0:8] + product[8:16]) + (product[16:24] + product[24:32])
                    )
            for k in range(REAL):
                grad[k : k + 1, lanes] = jnp.sum(total[k], axis=0, keepdims=True) * scale
        whole = grad[...]
        out[...] = fold(whole).astype(BF16)

    def reduce_gradient(phase, part, arrived):
        send_all("dp", phase, lambda o: part, lambda off: arrived.at[me_dp])
        arrived[me_dp] = part[...]
        wait_all(recv_sem, phase, arrived)
        return unfold(sum_slots(arrived))

    def send_squares(phase, whole, part, arrived):
        squares = jnp.sum(whole * whole, axis=1, keepdims=True)
        diagonal = iota((REAL, 128), 0) == iota((REAL, 128), 1)
        part[...] = jnp.sum(jnp.where(diagonal, squares, 0.0), axis=0, keepdims=True)
        send_all("cells", phase, lambda o: part, lambda off: arrived.at[me_cells])
        arrived[me_cells] = part[...]

    def inverse_scale(arrived):
        total = sum_slots(arrived)
        diagonal = iota((REAL, 128), 0) == iota((REAL, 128), 1)
        column = jnp.sum(jnp.where(diagonal, total, 0.0), axis=1, keepdims=True)
        return 1.0 / jnp.sqrt(column / cells_total + 1e-06)

    gradient(predicted, g1_s)
    first = reduce_gradient(2, g1_s, g1_r)
    send_squares(4, first, q1_s, q1_r)

    table = jnp.zeros((32 * REAL, 128), F32)
    for c in range(COMP):
        field = rc[c]
        scaled = [(field * first[k : k + 1]).astype(BF16) for k in range(REAL)]
        table = table + dot_nt(jnp.concatenate(scaled, axis=0), sc[c])
    spread = dot(split_halves(table * scale), is_source)
    change = jnp.concatenate(
        [
            jnp.sum(spread[32 * k : 32 * k + 32] * is_receiver, axis=0, keepdims=True)
            for k in range(REAL)
        ],
        axis=0,
    )
    dl_s[...] = fold(change).astype(BF16)
    send_all("cells", 3, lambda o: dl_s, lambda off: dl_r.at[me_cells])
    dl_r[me_cells] = dl_s[...]
    wait_all(recv_sem, 4, q1_r)
    inverse1 = inverse_scale(q1_r)
    wait_all(recv_sem, 3, dl_r)
    change = unfold(sum_slots(dl_r))
    gradient(predicted - 0.1 * (change * inverse1), g2_s)
    velocity = first * inverse1
    base = (start - 0.1 * velocity) - 0.1 * (0.9 * velocity)
    second = reduce_gradient(5, g2_s, g2_r)
    send_squares(6, second, q2_s, q2_r)
    wait_all(recv_sem, 6, q2_r)
    out_ref[...] = base - 0.1 * (second * inverse_scale(q2_r))

    for phase, ref in enumerate((data_r, tab_r, g1_r, dl_r, q1_r, g2_r, q2_r)):
        wait_all(send_sem, phase, ref)


def on_device(source, receiver, source_index, receiver_index, observed, noise, huber, start):
    cells = start.shape[0]
    n_data = source_index.shape[0]
    held = [
        pltpu.VMEM((source.shape[0] * COMP, cells), BF16),
        pltpu.VMEM((receiver.shape[0] * COMP, cells), BF16),
        pltpu.VMEM((1, n_data), jnp.int32),
        pltpu.VMEM((1, n_data), jnp.int32),
        pltpu.VMEM((1, n_data), F32),
        pltpu.VMEM((REAL, n_data), jnp.int32),
        pltpu.SMEM((REAL,), jnp.int32),
        pltpu.VMEM((cells // 128, 128), F32),
    ]

    def pair(shape, dtype):
        return [pltpu.VMEM(shape, dtype), pltpu.VMEM((GROUP,) + shape, dtype)]

    return pl.pallas_call(
        functools.partial(body, cells * GROUP),
        out_shape=jax.ShapeDtypeStruct((REAL, cells), F32),
        in_specs=[pl.BlockSpec(memory_space=pltpu.HBM)] * 8,
        out_specs=pl.BlockSpec(memory_space=pltpu.VMEM),
        scratch_shapes=held
        + [
            pltpu.VMEM((COMP, 128, cells), BF16),
            pltpu.VMEM((COMP, 32, cells), F32),
            pltpu.VMEM((REAL, cells), F32),
            pltpu.VMEM((4, 16, 128), F32),
            pltpu.VMEM((GROUP, 16, 128), F32),
        ]
        + pair((2, 8, 128), F32)
        + pair((16, cells // 2), BF16)
        + pair((16, n_data // 2), BF16)
        + pair((1, 128), F32)
        + pair((16, cells // 2), BF16)
        + pair((1, 128), F32)
        + [
            pltpu.SemaphoreType.DMA((7,)),
            pltpu.SemaphoreType.DMA((7,)),
            pltpu.SemaphoreType.DMA((8,)),
        ],
        compiler_params=pltpu.CompilerParams(collective_id=0, has_side_effects=True),
    )(
        source.reshape(-1, cells),
        receiver.reshape(-1, cells),
        source_index.reshape(1, n_data),
        receiver_index.reshape(1, n_data),
        observed.reshape(1, n_data),
        noise,
        huber,
        start.reshape(-1, 128),
    )


def solution(mesh):
    placed = (
        P(None, None, "cells"),
        P("dp", None, "cells"),
        P("dp"),
        P("dp"),
        P("dp"),
        P(None, "dp"),
        P(),
        P("cells"),
    )
    return jax.shard_map(
        on_device, mesh=mesh, in_specs=placed, out_specs=P(None, "cells"), check_vma=False
    )
```

```python
import functools
import math

import jax
import jax.numpy as jnp
from jax import lax
from jax.experimental import pallas as pl
from jax.experimental.pallas import tpu as pltpu
from jax.sharding import PartitionSpec as P

F32 = jnp.float32
BF16 = jnp.bfloat16
GROUP = 16
COMP = 8
REAL = 8
MESH = pl.DeviceIdType.MESH
FAR_FIRST = sorted(range(1, GROUP), key=lambda o: -min(o, GROUP - o))


def iota(shape, axis):
    return lax.broadcasted_iota(jnp.int32, shape, axis)


def dot(a, b):
    return jnp.dot(a, b, preferred_element_type=F32)


def dot_nt(a, b):
    return lax.dot_general(a, b, (((1,), (1,)), ((), ())), preferred_element_type=F32)


def split_halves(table):
    high = table.astype(BF16).astype(F32)
    return jnp.where(iota(table.shape, 1) < 64, high, table - high).astype(BF16)


def body(
    cells_total,
    *refs,
):
    given, out_ref, held, refs = refs[:8], refs[8], refs[9:17], refs[17:]
    src_ref, rec_ref, sidx_ref, ridx_ref, obs_ref, noise_ref, huber_ref, start_ref = held
    sc, rc, grad, data_s, data_r, tab_s, tab_r, g1_s, g1_r, dl_s, dl_r, q1_s, q1_r = refs[:13]
    g2_s, g2_r, q2_s, q2_r, send_sem, recv_sem, load_sem = refs[13:]
    me_dp = lax.axis_index("dp")
    me_cells = lax.axis_index("cells")
    cells = src_ref.shape[1]
    n_data = sidx_ref.shape[1]
    scale = 0.2 / math.sqrt(COMP * cells_total)

    def peer(axis, offset):
        me = me_dp if axis == "dp" else me_cells
        return lax.rem(me + offset, GROUP)

    barrier = pltpu.get_barrier_semaphore()

    for offset in FAR_FIRST:
        for axis in ("cells", "dp"):
            pl.semaphore_signal(
                barrier, inc=1, device_id={axis: peer(axis, offset)}, device_id_type=MESH
            )
    loads = [
        pltpu.make_async_copy(a, b, load_sem.at[n]) for n, (a, b) in enumerate(zip(given, held))
    ]
    for n in (1, 7, 0, 2, 3, 4, 5, 6):
        loads[n].start()

    def send_all(axis, phase, src_of, dst_of):
        for offset in FAR_FIRST:
            other = peer(axis, offset)
            pltpu.make_async_remote_copy(
                src_ref=src_of(other),
                dst_ref=dst_of(offset),
                send_sem=send_sem.at[phase],
                recv_sem=recv_sem.at[phase],
                device_id={axis: other},
                device_id_type=MESH,
            ).start()

    def wait_all(sem, phase, ref):
        part = ref.at[pl.ds(0, GROUP - 1)]
        pltpu.make_async_copy(part, part, sem.at[phase]).wait()

    pick = (
        (iota((128, 128), 0) % 16) * COMP + iota((128, 128), 0) // 16 == iota((128, 128), 1)
    ).astype(F32).astype(BF16)
    loads[1].wait()
    for chunk in range(2):
        rows = dot(pick, rec_ref[128 * chunk : 128 * chunk + 128, :])
        for c in range(COMP):
            part = rows[16 * c : 16 * c + 16, :]
            rc[c, 16 * chunk : 16 * chunk + 16, :] = part if c % 2 == 0 else -part
    loads[0].wait()
    zero_rows = jnp.zeros((16, cells), BF16)
    for chunk in range(3):
        rows = dot(pick, src_ref[128 * chunk : 128 * chunk + 128, :]).astype(BF16)
        for c in range(COMP):
            part = rows[16 * c : 16 * c + 16, :]
            sc[c, 16 * chunk : 16 * chunk + 16, :] = part
            sc[c, 64 + 16 * chunk : 80 + 16 * chunk, :] = part
    for c in range(COMP):
        sc[c, 48:64, :] = zero_rows
        sc[c, 112:128, :] = zero_rows

    loads[7].wait()
    start = jnp.concatenate([start_ref[n : n + 1, :] for n in range(cells // 128)], axis=1)
    start_half = start.astype(BF16).astype(F32)
    table = jnp.zeros((64, 128), F32)
    for c in range(COMP):
        exact = rc[c] * start_half
        high = exact.astype(BF16)
        low = (exact - high.astype(F32)).astype(BF16)
        table = table + dot_nt(jnp.concatenate([high, low], axis=0), sc[c])
    table = (table[0:32] + table[32:64]) * scale
    left = iota((8, 128), 1) < 64
    tab_s[0] = jnp.where(left, table[0:8], table[8:16])
    tab_s[1] = jnp.where(left, table[16:24], table[24:32])

    pl.semaphore_wait(barrier, 2 * (GROUP - 1))
    send_all("cells", 1, lambda o: tab_s, lambda off: tab_r.at[off - 1])

    for n in range(2, 7):
        loads[n].wait()
    owner = ridx_ref[...] // 32
    local = ridx_ref[...] % 32
    member = (iota((16, n_data), 0) == owner).astype(F32)
    before = (iota((n_data, n_data), 0) < iota((n_data, n_data), 1)).astype(F32).astype(BF16)
    rank = jnp.sum(member * dot(member.astype(BF16), before), axis=0, keepdims=True)
    place = (128 * (owner // 4) + 32 * ((owner + me_dp) % 4)).astype(F32) + rank
    move = (iota((n_data, n_data), 0).astype(F32) == place).astype(F32).astype(BF16)
    shifted = obs_ref[...] + noise_ref[...].astype(F32) / 4096.0
    high = shifted.astype(BF16).astype(F32)
    middle = (shifted - high).astype(BF16).astype(F32)
    low = shifted - high - middle
    row8 = iota((8, n_data), 0)
    index_rows = jnp.where(
        row8 == 0,
        sidx_ref[...].astype(F32),
        jnp.where(row8 == 1, local.astype(F32), 0.0),
    )
    moved = dot_nt(jnp.concatenate([high, middle, low, index_rows], axis=0).astype(BF16), move)
    shifted = moved[0:8] + moved[8:16] + moved[16:24]
    for t in range(4):
        data_s[t, 0:8, :] = shifted[:, 128 * t : 128 * t + 128]
        data_s[t, 8:16, :] = moved[24:32, 128 * t : 128 * t + 128]
    send_all("dp", 0, lambda o: data_s.at[o // 4], lambda off: data_r.at[off - 1])
    data_r[GROUP - 1] = data_s[me_dp // 4]
    wait_all(recv_sem, 0, data_r)
    quarter = iota((16, 128), 1) // 32
    tiles = []
    for t in range(4):
        tile = data_r[4 * t]
        for o in range(4 * t + 2, 4 * t + 5):
            here = lax.rem(2 * me_dp + 32 - o, 4)
            tile = jnp.where(quarter == here, data_r[o - 1], tile)
        tiles.append(tile)
    data = jnp.concatenate(tiles, axis=1)
    shifted = data[0:8]
    source = data[8:9].astype(jnp.int32)
    receiver = data[9:10].astype(jnp.int32)
    is_source = (iota((128, n_data), 0) % 64 == source).astype(F32).astype(BF16)
    is_receiver = (iota((32, n_data), 0) == receiver).astype(F32)
    limit = jnp.zeros((REAL, n_data), F32)
    for k in range(REAL):
        limit = jnp.where(row8 == k, huber_ref[k].astype(F32) / 16.0, limit)

    wait_all(recv_sem, 1, tab_r)
    packed = tab_s[...]
    for o in range(GROUP - 1):
        packed = packed + tab_r[o]
    rows = []
    for t in range(2):
        here = packed[t]
        turned = pltpu.roll(here, 64, 1)
        rows.append(jnp.where(left, here, turned))
        rows.append(jnp.where(left, turned, here))
    spread = dot(split_halves(jnp.concatenate(rows, axis=0)), is_source)
    predicted = jnp.sum(spread * is_receiver, axis=0, keepdims=True)

    def fold(x):
        half = x.shape[1] // 2
        return jnp.concatenate([x[:, :half], x[:, half:]], axis=0)

    def unfold(x):
        half = x.shape[0] // 2
        return jnp.concatenate([x[:half], x[half:]], axis=1)

    def sum_slots(arrived):
        parts = [arrived[o].astype(F32) for o in range(GROUP)]
        while len(parts) > 1:
            parts = [a + b for a, b in zip(parts[::2], parts[1::2])]
        return parts[0]

    def gradient(predicted, out):
        weighted = jnp.clip(predicted - shifted, -limit, limit).astype(BF16).astype(F32)
        spread = [(weighted[k : k + 1, :] * is_receiver).astype(BF16) for k in range(REAL)]
        pairs = split_halves(dot_nt(jnp.concatenate(spread, axis=0), is_source))
        for b in range(cells // 256):
            lanes = slice(256 * b, 256 * b + 256)
            total = [jnp.zeros((8, 256), F32) for k in range(REAL)]
            for c in range(COMP):
                mixed = dot(pairs, sc[c, :, lanes])
                field = rc[c, :, lanes]
                for k in range(REAL):
                    product = mixed[32 * k : 32 * k + 32] * field
                    total[k] = total[k] + (
                        (product[0:8] + product[8:16]) + (product[16:24] + product[24:32])
                    )
            for k in range(REAL):
                grad[k : k + 1, lanes] = jnp.sum(total[k], axis=0, keepdims=True) * scale
        whole = grad[...]
        out[...] = fold(whole).astype(BF16)

    def reduce_gradient(phase, part, arrived):
        send_all("dp", phase, lambda o: part, lambda off: arrived.at[me_dp])
        arrived[me_dp] = part[...]
        wait_all(recv_sem, phase, arrived)
        return unfold(sum_slots(arrived))

    def send_squares(phase, whole, part, arrived):
        squares = jnp.sum(whole * whole, axis=1, keepdims=True)
        diagonal = iota((REAL, 128), 0) == iota((REAL, 128), 1)
        part[...] = jnp.sum(jnp.where(diagonal, squares, 0.0), axis=0, keepdims=True)
        send_all("cells", phase, lambda o: part, lambda off: arrived.at[me_cells])
        arrived[me_cells] = part[...]

    def inverse_scale(arrived):
        total = sum_slots(arrived)
        diagonal = iota((REAL, 128), 0) == iota((REAL, 128), 1)
        column = jnp.sum(jnp.where(diagonal, total, 0.0), axis=1, keepdims=True)
        return 1.0 / jnp.sqrt(column / cells_total + 1e-06)

    gradient(predicted, g1_s)
    first = reduce_gradient(2, g1_s, g1_r)
    send_squares(4, first, q1_s, q1_r)

    table = jnp.zeros((32 * REAL, 128), F32)
    for c in range(COMP):
        field = rc[c]
        scaled = [(field * first[k : k + 1]).astype(BF16) for k in range(REAL)]
        table = table + dot_nt(jnp.concatenate(scaled, axis=0), sc[c])
    spread = dot(split_halves(table * scale), is_source)
    change = jnp.concatenate(
        [
            jnp.sum(spread[32 * k : 32 * k + 32] * is_receiver, axis=0, keepdims=True)
            for k in range(REAL)
        ],
        axis=0,
    )
    dl_s[...] = fold(change).astype(BF16)
    send_all("cells", 3, lambda o: dl_s, lambda off: dl_r.at[me_cells])
    dl_r[me_cells] = dl_s[...]
    wait_all(recv_sem, 4, q1_r)
    inverse1 = inverse_scale(q1_r)
    wait_all(recv_sem, 3, dl_r)
    change = unfold(sum_slots(dl_r))
    gradient(predicted - 0.1 * (change * inverse1), g2_s)
    velocity = first * inverse1
    base = (start - 0.1 * velocity) - 0.1 * (0.9 * velocity)
    second = reduce_gradient(5, g2_s, g2_r)
    send_squares(6, second, q2_s, q2_r)
    wait_all(recv_sem, 6, q2_r)
    out_ref[...] = base - 0.1 * (second * inverse_scale(q2_r))

    for phase, ref in enumerate((data_r, tab_r, g1_r, dl_r, q1_r, g2_r, q2_r)):
        wait_all(send_sem, phase, ref)


def on_device(source, receiver, source_index, receiver_index, observed, noise, huber, start):
    cells = start.shape[0]
    n_data = source_index.shape[0]
    held = [
        pltpu.VMEM((source.shape[0] * COMP, cells), BF16),
        pltpu.VMEM((receiver.shape[0] * COMP, cells), BF16),
        pltpu.VMEM((1, n_data), jnp.int32),
        pltpu.VMEM((1, n_data), jnp.int32),
        pltpu.VMEM((1, n_data), F32),
        pltpu.VMEM((REAL, n_data), jnp.int32),
        pltpu.SMEM((REAL,), jnp.int32),
        pltpu.VMEM((cells // 128, 128), F32),
    ]

    def pair(shape, dtype):
        return [pltpu.VMEM(shape, dtype), pltpu.VMEM((GROUP,) + shape, dtype)]

    return pl.pallas_call(
        functools.partial(body, cells * GROUP),
        out_shape=pltpu.VMEM((REAL, cells), F32),
        in_specs=[pl.BlockSpec(memory_space=pltpu.HBM)] * 8,
        out_specs=pl.BlockSpec(memory_space=pltpu.VMEM),
        scratch_shapes=held
        + [
            pltpu.VMEM((COMP, 128, cells), BF16),
            pltpu.VMEM((COMP, 32, cells), F32),
            pltpu.VMEM((REAL, cells), F32),
            pltpu.VMEM((4, 16, 128), F32),
            pltpu.VMEM((GROUP, 16, 128), F32),
        ]
        + pair((2, 8, 128), F32)
        + pair((16, cells // 2), BF16)
        + pair((16, n_data // 2), BF16)
        + pair((1, 128), F32)
        + pair((16, cells // 2), BF16)
        + pair((1, 128), F32)
        + [
            pltpu.SemaphoreType.DMA((7,)),
            pltpu.SemaphoreType.DMA((7,)),
            pltpu.SemaphoreType.DMA((8,)),
        ],
        compiler_params=pltpu.CompilerParams(collective_id=0, has_side_effects=True),
    )(
        source.reshape(-1, cells),
        receiver.reshape(-1, cells),
        source_index.reshape(1, n_data),
        receiver_index.reshape(1, n_data),
        observed.reshape(1, n_data),
        noise,
        huber,
        start.reshape(-1, 128),
    )


def solution(mesh):
    placed = (
        P(None, None, "cells"),
        P("dp", None, "cells"),
        P("dp"),
        P("dp"),
        P("dp"),
        P(None, "dp"),
        P(),
        P("cells"),
    )
    return jax.shard_map(
        on_device, mesh=mesh, in_specs=placed, out_specs=P(None, "cells"), check_vma=False
    )
```

```python
import functools
import math

import jax
import jax.numpy as jnp
from jax import lax
from jax.experimental import pallas as pl
from jax.experimental.pallas import tpu as pltpu
from jax.sharding import PartitionSpec as P

F32 = jnp.float32
BF16 = jnp.bfloat16
GROUP = 16
COMP = 8
REAL = 8
SOURCES = 48
RECEIVERS = 32
MESH = pl.DeviceIdType.MESH
FAR_FIRST = sorted(range(1, GROUP), key=lambda o: -min(o, GROUP - o))


def iota(shape, axis):
    return lax.broadcasted_iota(jnp.int32, shape, axis)


def dot(a, b):
    return jnp.dot(a, b, preferred_element_type=F32)


def dot_nt(a, b):
    return lax.dot_general(a, b, (((1,), (1,)), ((), ())), preferred_element_type=F32)


def split_halves(table):
    high = table.astype(BF16).astype(F32)
    return jnp.where(iota(table.shape, 1) < 64, high, table - high).astype(BF16)


def body(
    cells_total,
    *refs,
):
    given, out_ref, held, refs = refs[:8], refs[8], refs[9:17], refs[17:]
    src_ref, rec_ref, sidx_ref, ridx_ref, obs_ref, noise_ref, huber_ref, start_ref = held
    sc, sf, rc, rk, ka, kd, data_s, data_r, tab_s, tab_r, g1_s, g1_r, dl_s, dl_r, q1_s, q1_r = refs[:16]
    g2_s, g2_r, q2_s, q2_r, send_sem, recv_sem, load_sem = refs[16:]
    me_dp = lax.axis_index("dp")
    me_cells = lax.axis_index("cells")
    cells = src_ref.shape[1]
    n_data = sidx_ref.shape[1]
    scale = 0.2 / math.sqrt(COMP * cells_total)

    def peer(axis, offset):
        me = me_dp if axis == "dp" else me_cells
        return lax.rem(me + offset, GROUP)

    barrier = pltpu.get_barrier_semaphore()

    for offset in FAR_FIRST:
        for axis in ("cells", "dp"):
            pl.semaphore_signal(
                barrier, inc=1, device_id={axis: peer(axis, offset)}, device_id_type=MESH
            )
    loads = [
        pltpu.make_async_copy(a, b, load_sem.at[n]) for n, (a, b) in enumerate(zip(given, held))
    ]
    for n in (1, 7, 0, 2, 3, 4, 5, 6):
        loads[n].start()

    def send_all(axis, phase, src_of, dst_of):
        for offset in FAR_FIRST:
            other = peer(axis, offset)
            pltpu.make_async_remote_copy(
                src_ref=src_of(other),
                dst_ref=dst_of(offset),
                send_sem=send_sem.at[phase],
                recv_sem=recv_sem.at[phase],
                device_id={axis: other},
                device_id_type=MESH,
            ).start()

    def wait_all(sem, phase, ref):
        part = ref.at[pl.ds(0, GROUP - 1)]
        pltpu.make_async_copy(part, part, sem.at[phase]).wait()

    pick = (
        (iota((128, 128), 0) % 16) * COMP + iota((128, 128), 0) // 16 == iota((128, 128), 1)
    ).astype(F32).astype(BF16)
    loads[1].wait()
    for chunk in range(2):
        rows = dot(pick, rec_ref[128 * chunk : 128 * chunk + 128, :])
        for c in range(COMP):
            part = rows[16 * c : 16 * c + 16, :]
            rc[c, 16 * chunk : 16 * chunk + 16, :] = part if c % 2 == 0 else -part
    loads[0].wait()
    zero_rows = jnp.zeros((16, cells), BF16)
    for chunk in range(3):
        rows = dot(pick, src_ref[128 * chunk : 128 * chunk + 128, :])
        for c in range(COMP):
            part = rows[16 * c : 16 * c + 16, :]
            sf[c, 16 * chunk : 16 * chunk + 16, :] = part
            part = part.astype(BF16)
            sc[c, 16 * chunk : 16 * chunk + 16, :] = part
            sc[c, 64 + 16 * chunk : 80 + 16 * chunk, :] = part
    for c in range(COMP):
        sc[c, 48:64, :] = zero_rows
        sc[c, 112:128, :] = zero_rows

    loads[7].wait()
    start = jnp.concatenate([start_ref[n : n + 1, :] for n in range(cells // 128)], axis=1)
    start_half = start.astype(BF16).astype(F32)
    table = jnp.zeros((64, 128), F32)
    for c in range(COMP):
        exact = rc[c] * start_half
        high = exact.astype(BF16)
        low = (exact - high.astype(F32)).astype(BF16)
        table = table + dot_nt(jnp.concatenate([high, low], axis=0), sc[c])
    table = (table[0:32] + table[32:64]) * scale
    left = iota((8, 128), 1) < 64
    tab_s[0] = jnp.where(left, table[0:8], table[8:16])
    tab_s[1] = jnp.where(left, table[16:24], table[24:32])

    for n in range(2, 7):
        loads[n].wait()
    owner = ridx_ref[...] // 32
    local = ridx_ref[...] % 32
    member = (iota((16, n_data), 0) == owner).astype(F32)
    before = (iota((n_data, n_data), 0) < iota((n_data, n_data), 1)).astype(F32).astype(BF16)
    rank = jnp.sum(member * dot(member.astype(BF16), before), axis=0, keepdims=True)
    place = (128 * (owner // 4) + 32 * ((owner + me_dp) % 4)).astype(F32) + rank
    move = (iota((n_data, n_data), 0).astype(F32) == place).astype(F32).astype(BF16)
    shifted = obs_ref[...] + noise_ref[...].astype(F32) / 4096.0
    high = shifted.astype(BF16).astype(F32)
    middle = (shifted - high).astype(BF16).astype(F32)
    low = shifted - high - middle
    row8 = iota((8, n_data), 0)
    index_rows = jnp.where(
        row8 == 0,
        sidx_ref[...].astype(F32),
        jnp.where(row8 == 1, local.astype(F32), 0.0),
    )
    moved = dot_nt(jnp.concatenate([high, middle, low, index_rows], axis=0).astype(BF16), move)
    shifted = moved[0:8] + moved[8:16] + moved[16:24]
    for t in range(4):
        data_s[t, 0:8, :] = shifted[:, 128 * t : 128 * t + 128]
        data_s[t, 8:16, :] = moved[24:32, 128 * t : 128 * t + 128]
    pl.semaphore_wait(barrier, 2 * (GROUP - 1))
    send_all("cells", 1, lambda o: tab_s, lambda off: tab_r.at[off - 1])
    send_all("dp", 0, lambda o: data_s.at[o // 4], lambda off: data_r.at[off - 1])

    signs = jnp.where(iota((COMP, cells), 0) % 2 == 0, scale, -scale)
    for r in range(RECEIVERS):
        rk[r] = rec_ref[COMP * r : COMP * r + COMP, :].astype(F32) * signs

    def form(r, carry):
        for n in range(cells // 128):
            lanes = slice(128 * n, 128 * n + 128)
            factors = rk[r, :, lanes]
            rows = sf[0, :, lanes] * factors[0:1]
            for c in range(1, COMP):
                rows = rows + sf[c, :, lanes] * factors[c : c + 1]
            ka[r, :, lanes] = rows.astype(BF16)
        return carry

    lax.fori_loop(0, RECEIVERS, form, 0)

    data_r[GROUP - 1] = data_s[me_dp // 4]
    wait_all(recv_sem, 0, data_r)
    quarter = iota((16, 128), 1) // 32
    tiles = []
    for t in range(4):
        tile = data_r[4 * t]
        for o in range(4 * t + 2, 4 * t + 5):
            here = lax.rem(2 * me_dp + 32 - o, 4)
            tile = jnp.where(quarter == here, data_r[o - 1], tile)
        tiles.append(tile)
    data = jnp.concatenate(tiles, axis=1)
    shifted = data[0:8]
    column = jnp.transpose(data[8:16])
    code = column[:, 1:2] * SOURCES + column[:, 0:1]
    pairs = RECEIVERS * SOURCES
    chosen = (iota((n_data, pairs), 1).astype(F32) == code).astype(F32).astype(BF16)
    kd[...] = dot(chosen, ka[...].reshape(pairs, cells)).astype(BF16)
    source = data[8:9].astype(jnp.int32)
    receiver = data[9:10].astype(jnp.int32)
    is_source = (iota((128, n_data), 0) % 64 == source).astype(F32).astype(BF16)
    is_receiver = (iota((32, n_data), 0) == receiver).astype(F32)
    limit = jnp.zeros((REAL, n_data), F32)
    for k in range(REAL):
        limit = jnp.where(row8 == k, huber_ref[k].astype(F32) / 16.0, limit)

    wait_all(recv_sem, 1, tab_r)
    packed = tab_s[...]
    for o in range(GROUP - 1):
        packed = packed + tab_r[o]
    rows = []
    for t in range(2):
        here = packed[t]
        turned = pltpu.roll(here, 64, 1)
        rows.append(jnp.where(left, here, turned))
        rows.append(jnp.where(left, turned, here))
    spread = dot(split_halves(jnp.concatenate(rows, axis=0)), is_source)
    predicted = jnp.sum(spread * is_receiver, axis=0, keepdims=True)

    def fold(x):
        half = x.shape[1] // 2
        return jnp.concatenate([x[:, :half], x[:, half:]], axis=0)

    def unfold(x):
        half = x.shape[0] // 2
        return jnp.concatenate([x[:half], x[half:]], axis=1)

    def sum_slots(arrived):
        parts = [arrived[o].astype(F32) for o in range(GROUP)]
        while len(parts) > 1:
            parts = [a + b for a, b in zip(parts[::2], parts[1::2])]
        return parts[0]

    def gradient(predicted, out):
        weighted = jnp.clip(predicted - shifted, -limit, limit).astype(BF16)
        out[...] = fold(dot(weighted, kd[...])).astype(BF16)

    def reduce_gradient(phase, part, arrived):
        send_all("dp", phase, lambda o: part, lambda off: arrived.at[me_dp])
        arrived[me_dp] = part[...]
        wait_all(recv_sem, phase, arrived)
        return unfold(sum_slots(arrived))

    def send_squares(phase, whole, part, arrived):
        squares = jnp.sum(whole * whole, axis=1, keepdims=True)
        diagonal = iota((REAL, 128), 0) == iota((REAL, 128), 1)
        part[...] = jnp.sum(jnp.where(diagonal, squares, 0.0), axis=0, keepdims=True)
        send_all("cells", phase, lambda o: part, lambda off: arrived.at[me_cells])
        arrived[me_cells] = part[...]

    def inverse_scale(arrived):
        total = sum_slots(arrived)
        diagonal = iota((REAL, 128), 0) == iota((REAL, 128), 1)
        column = jnp.sum(jnp.where(diagonal, total, 0.0), axis=1, keepdims=True)
        return 1.0 / jnp.sqrt(column / cells_total + 1e-06)

    gradient(predicted, g1_s)
    first = reduce_gradient(2, g1_s, g1_r)
    send_squares(4, first, q1_s, q1_r)

    high = first.astype(BF16).astype(F32)
    both = jnp.concatenate([high, first - high], axis=0).astype(BF16)
    both = dot_nt(both, kd[...])
    change = both[:REAL] + both[REAL:]
    dl_s[...] = fold(change).astype(BF16)
    send_all("cells", 3, lambda o: dl_s, lambda off: dl_r.at[me_cells])
    dl_r[me_cells] = dl_s[...]
    wait_all(recv_sem, 4, q1_r)
    inverse1 = inverse_scale(q1_r)
    wait_all(recv_sem, 3, dl_r)
    change = unfold(sum_slots(dl_r))
    gradient(predicted - 0.1 * (change * inverse1), g2_s)
    velocity = first * inverse1
    base = (start - 0.1 * velocity) - 0.1 * (0.9 * velocity)
    second = reduce_gradient(5, g2_s, g2_r)
    send_squares(6, second, q2_s, q2_r)
    wait_all(recv_sem, 6, q2_r)
    out_ref[...] = base - 0.1 * (second * inverse_scale(q2_r))

    for phase, ref in enumerate((data_r, tab_r, g1_r, dl_r, q1_r, g2_r, q2_r)):
        wait_all(send_sem, phase, ref)


def on_device(source, receiver, source_index, receiver_index, observed, noise, huber, start):
    cells = start.shape[0]
    n_data = source_index.shape[0]
    held = [
        pltpu.VMEM((source.shape[0] * COMP, cells), BF16),
        pltpu.VMEM((receiver.shape[0] * COMP, cells), BF16),
        pltpu.VMEM((1, n_data), jnp.int32),
        pltpu.VMEM((1, n_data), jnp.int32),
        pltpu.VMEM((1, n_data), F32),
        pltpu.VMEM((REAL, n_data), jnp.int32),
        pltpu.SMEM((REAL,), jnp.int32),
        pltpu.VMEM((cells // 128, 128), F32),
    ]

    def pair(shape, dtype):
        return [pltpu.VMEM(shape, dtype), pltpu.VMEM((GROUP,) + shape, dtype)]

    return pl.pallas_call(
        functools.partial(body, cells * GROUP),
        out_shape=pltpu.VMEM((REAL, cells), F32),
        in_specs=[pl.BlockSpec(memory_space=pltpu.HBM)] * 8,
        out_specs=pl.BlockSpec(memory_space=pltpu.VMEM),
        scratch_shapes=held
        + [
            pltpu.VMEM((COMP, 128, cells), BF16),
            pltpu.VMEM((COMP, SOURCES, cells), F32),
            pltpu.VMEM((COMP, RECEIVERS, cells), F32),
            pltpu.VMEM((RECEIVERS, COMP, cells), F32),
            pltpu.VMEM((RECEIVERS, SOURCES, cells), BF16),
            pltpu.VMEM((n_data, cells), BF16),
            pltpu.VMEM((4, 16, 128), F32),
            pltpu.VMEM((GROUP, 16, 128), F32),
        ]
        + pair((2, 8, 128), F32)
        + pair((16, cells // 2), BF16)
        + pair((16, n_data // 2), BF16)
        + pair((1, 128), F32)
        + pair((16, cells // 2), BF16)
        + pair((1, 128), F32)
        + [
            pltpu.SemaphoreType.DMA((7,)),
            pltpu.SemaphoreType.DMA((7,)),
            pltpu.SemaphoreType.DMA((8,)),
        ],
        compiler_params=pltpu.CompilerParams(collective_id=0, has_side_effects=True),
    )(
        source.reshape(-1, cells),
        receiver.reshape(-1, cells),
        source_index.reshape(1, n_data),
        receiver_index.reshape(1, n_data),
        observed.reshape(1, n_data),
        noise,
        huber,
        start.reshape(-1, 128),
    )


def solution(mesh):
    placed = (
        P(None, None, "cells"),
        P("dp", None, "cells"),
        P("dp"),
        P("dp"),
        P("dp"),
        P(None, "dp"),
        P(),
        P("cells"),
    )
    return jax.shard_map(
        on_device, mesh=mesh, in_specs=placed, out_specs=P(None, "cells"), check_vma=False
    )
```

```python
import functools
import math

import jax
import jax.numpy as jnp
from jax import lax
from jax.experimental import pallas as pl
from jax.experimental.pallas import tpu as pltpu
from jax.sharding import PartitionSpec as P

F32 = jnp.float32
BF16 = jnp.bfloat16
GROUP = 16
COMP = 8
REAL = 8
SOURCES = 48
RECEIVERS = 32
MESH = pl.DeviceIdType.MESH
FAR_FIRST = sorted(range(1, GROUP), key=lambda o: -min(o, GROUP - o))


def iota(shape, axis):
    return lax.broadcasted_iota(jnp.int32, shape, axis)


def dot(a, b):
    return jnp.dot(a, b, preferred_element_type=F32)


def dot_nt(a, b):
    return lax.dot_general(a, b, (((1,), (1,)), ((), ())), preferred_element_type=F32)


def split_halves(table):
    high = table.astype(BF16).astype(F32)
    return jnp.where(iota(table.shape, 1) < 64, high, table - high).astype(BF16)


def body(
    cells_total,
    *refs,
):
    given, out_ref, held, refs = refs[:8], refs[8], refs[9:17], refs[17:]
    src_ref, rec_ref, sidx_ref, ridx_ref, obs_ref, noise_ref, huber_ref, start_ref = held
    sf, rk, ka, kd, oh, data_s, data_r, tab_s, tab_r, g1_s, g1_r, dl_s, dl_r, q1_s, q1_r = refs[:15]
    g2_s, g2_r, q2_s, q2_r, send_sem, recv_sem, load_sem = refs[15:]
    me_dp = lax.axis_index("dp")
    me_cells = lax.axis_index("cells")
    cells = src_ref.shape[1]
    n_data = sidx_ref.shape[1]
    scale = 0.2 / math.sqrt(COMP * cells_total)

    def peer(axis, offset):
        me = me_dp if axis == "dp" else me_cells
        return lax.rem(me + offset, GROUP)

    barrier = pltpu.get_barrier_semaphore()

    def greet(axis, offsets):
        for offset in offsets:
            pl.semaphore_signal(
                barrier, inc=1, device_id={axis: peer(axis, offset)}, device_id_type=MESH
            )

    greet("cells", FAR_FIRST[:8])
    loads = [
        pltpu.make_async_copy(a, b, load_sem.at[n]) for n, (a, b) in enumerate(zip(given, held))
    ]
    for n in (3, 2, 4, 5, 1, 7, 0, 6):
        loads[n].start()
    greet("cells", FAR_FIRST[8:])
    greet("dp", FAR_FIRST)

    def send_all(axis, phase, src_of, dst_of):
        for offset in FAR_FIRST:
            other = peer(axis, offset)
            pltpu.make_async_remote_copy(
                src_ref=src_of(other),
                dst_ref=dst_of(offset),
                send_sem=send_sem.at[phase],
                recv_sem=recv_sem.at[phase],
                device_id={axis: other},
                device_id_type=MESH,
            ).start()

    def wait_all(sem, phase, ref):
        part = ref.at[pl.ds(0, GROUP - 1)]
        pltpu.make_async_copy(part, part, sem.at[phase]).wait()

    for n in range(2, 7):
        loads[n].wait()
    owner = ridx_ref[...] // 32
    local = ridx_ref[...] % 32
    member = (iota((16, n_data), 0) == owner).astype(F32)
    before = (iota((n_data, n_data), 0) < iota((n_data, n_data), 1)).astype(F32).astype(BF16)
    rank = jnp.sum(member * dot(member.astype(BF16), before), axis=0, keepdims=True)
    place = (128 * (owner // 4) + 32 * ((owner + me_dp) % 4)).astype(F32) + rank
    move = (iota((n_data, n_data), 0).astype(F32) == place).astype(F32).astype(BF16)
    shifted = obs_ref[...] + noise_ref[...].astype(F32) / 4096.0
    high = shifted.astype(BF16).astype(F32)
    middle = (shifted - high).astype(BF16).astype(F32)
    low = shifted - high - middle
    row8 = iota((8, n_data), 0)
    index_rows = jnp.where(
        row8 == 0,
        sidx_ref[...].astype(F32),
        jnp.where(row8 == 1, local.astype(F32), 0.0),
    )
    moved = dot_nt(jnp.concatenate([high, middle, low, index_rows], axis=0).astype(BF16), move)
    shifted = moved[0:8] + moved[8:16] + moved[16:24]
    for t in range(4):
        data_s[t, 0:8, :] = shifted[:, 128 * t : 128 * t + 128]
        data_s[t, 8:16, :] = moved[24:32, 128 * t : 128 * t + 128]

    for n in (1, 7):
        loads[n].wait()
    start = jnp.concatenate([start_ref[n : n + 1, :] for n in range(cells // 128)], axis=1)
    exact = rec_ref[...].astype(F32) * start.astype(BF16).astype(F32)
    high = exact.astype(BF16)
    low = (exact - high.astype(F32)).astype(BF16)
    loads[0].wait()
    cross = dot_nt(high, src_ref[...]) + dot_nt(low, src_ref[...])
    shape = (COMP, SOURCES * COMP)
    odd = iota(shape, 0) % 2
    keep = jnp.where(iota(shape, 1) % COMP == iota(shape, 0), 1.0 - 2.0 * odd.astype(F32), 0.0)
    table = jnp.concatenate(
        [
            jnp.sum(cross[COMP * r : COMP * r + COMP] * keep, axis=0, keepdims=True)
            for r in range(RECEIVERS)
        ],
        axis=0,
    )
    high = table.astype(BF16)
    low = (table - high.astype(F32)).astype(BF16)
    shape = (SOURCES * COMP, 128)
    group = (iota(shape, 0) // COMP == iota(shape, 1) % 64).astype(F32).astype(BF16)
    table = dot(jnp.concatenate([high, low], axis=0), group)
    table = (table[:RECEIVERS] + table[RECEIVERS:]) * scale
    left = iota((8, 128), 1) < 64
    tab_s[0] = jnp.where(left, table[0:8], table[8:16])
    tab_s[1] = jnp.where(left, table[16:24], table[24:32])

    pl.semaphore_wait(barrier, 2 * (GROUP - 1))
    send_all("dp", 0, lambda o: data_s.at[o // 4], lambda off: data_r.at[off - 1])
    send_all("cells", 1, lambda o: tab_s, lambda off: tab_r.at[off - 1])

    pick = (
        (iota((128, 128), 0) % 16) * COMP + iota((128, 128), 0) // 16 == iota((128, 128), 1)
    ).astype(F32).astype(BF16)
    for chunk in range(3):
        rows = dot(pick, src_ref[128 * chunk : 128 * chunk + 128, :])
        for c in range(COMP):
            sf[c, 16 * chunk : 16 * chunk + 16, :] = rows[16 * c : 16 * c + 16, :]

    signs = jnp.where(iota((COMP, cells), 0) % 2 == 0, scale, -scale)
    for r in range(RECEIVERS):
        rk[r] = rec_ref[COMP * r : COMP * r + COMP, :].astype(F32) * signs

    def form(r, carry):
        for n in range(cells // 128):
            lanes = slice(128 * n, 128 * n + 128)
            factors = rk[r, :, lanes]
            rows = sf[0, :, lanes] * factors[0:1]
            for c in range(1, COMP):
                rows = rows + sf[c, :, lanes] * factors[c : c + 1]
            ka[r, :, lanes] = rows.astype(BF16)
        return carry

    lax.fori_loop(0, RECEIVERS, form, 0)

    data_r[GROUP - 1] = data_s[me_dp // 4]
    wait_all(recv_sem, 0, data_r)
    quarter = iota((16, 128), 1) // 32
    tiles = []
    for t in range(4):
        tile = data_r[4 * t]
        for o in range(4 * t + 2, 4 * t + 5):
            here = lax.rem(2 * me_dp + 32 - o, 4)
            tile = jnp.where(quarter == here, data_r[o - 1], tile)
        tiles.append(tile)
    data = jnp.concatenate(tiles, axis=1)
    shifted = data[0:8]
    column = jnp.transpose(data[8:16])
    code = column[:, 1:2] * SOURCES + column[:, 0:1]
    pairs = RECEIVERS * SOURCES
    oh[...] = (iota((n_data, pairs), 1).astype(F32) == code).astype(F32).astype(BF16)
    source = data[8:9].astype(jnp.int32)
    receiver = data[9:10].astype(jnp.int32)
    is_source = (iota((128, n_data), 0) % 64 == source).astype(F32).astype(BF16)
    is_receiver = (iota((32, n_data), 0) == receiver).astype(F32)
    limit = jnp.zeros((REAL, n_data), F32)
    for k in range(REAL):
        limit = jnp.where(row8 == k, huber_ref[k].astype(F32) / 16.0, limit)

    wait_all(recv_sem, 1, tab_r)
    packed = tab_s[...]
    for o in range(GROUP - 1):
        packed = packed + tab_r[o]
    rows = []
    for t in range(2):
        here = packed[t]
        turned = pltpu.roll(here, 64, 1)
        rows.append(jnp.where(left, here, turned))
        rows.append(jnp.where(left, turned, here))
    spread = dot(split_halves(jnp.concatenate(rows, axis=0)), is_source)
    predicted = jnp.sum(spread * is_receiver, axis=0, keepdims=True)

    def fold(x):
        half = x.shape[1] // 2
        return jnp.concatenate([x[:, :half], x[:, half:]], axis=0)

    def unfold(x):
        half = x.shape[0] // 2
        return jnp.concatenate([x[:half], x[half:]], axis=1)

    def sum_slots(arrived):
        parts = [arrived[o].astype(F32) for o in range(GROUP)]
        while len(parts) > 1:
            parts = [a + b for a, b in zip(parts[::2], parts[1::2])]
        return parts[0]

    def two_parts(x):
        high = x.astype(BF16).astype(F32)
        return jnp.concatenate([high, x - high], axis=0).astype(BF16)

    def weigh(predicted):
        return jnp.clip(predicted - shifted, -limit, limit).astype(BF16)

    def reduce_gradient(phase, whole, part, arrived, meanwhile):
        part[...] = fold(whole).astype(BF16)
        send_all("dp", phase, lambda o: part, lambda off: arrived.at[me_dp])
        arrived[me_dp] = part[...]
        meanwhile()
        wait_all(recv_sem, phase, arrived)
        return unfold(sum_slots(arrived))

    def send_squares(phase, whole, part, arrived):
        squares = jnp.sum(whole * whole, axis=1, keepdims=True)
        diagonal = iota((REAL, 128), 0) == iota((REAL, 128), 1)
        part[...] = jnp.sum(jnp.where(diagonal, squares, 0.0), axis=0, keepdims=True)
        send_all("cells", phase, lambda o: part, lambda off: arrived.at[me_cells])
        arrived[me_cells] = part[...]

    def inverse_scale(arrived):
        total = sum_slots(arrived)
        diagonal = iota((REAL, 128), 0) == iota((REAL, 128), 1)
        column = jnp.sum(jnp.where(diagonal, total, 0.0), axis=1, keepdims=True)
        return 1.0 / jnp.sqrt(column / cells_total + 1e-06)

    def pick_rows():
        kd[...] = dot(oh[...], ka[...].reshape(pairs, cells)).astype(BF16)

    both = dot(two_parts(dot(weigh(predicted), oh[...])), ka[...].reshape(pairs, cells))
    first = reduce_gradient(2, both[:REAL] + both[REAL:], g1_s, g1_r, pick_rows)
    send_squares(4, first, q1_s, q1_r)

    both = dot_nt(two_parts(first), kd[...])
    change = both[:REAL] + both[REAL:]
    dl_s[...] = fold(change).astype(BF16)
    send_all("cells", 3, lambda o: dl_s, lambda off: dl_r.at[me_cells])
    dl_r[me_cells] = dl_s[...]
    wait_all(recv_sem, 4, q1_r)
    inverse1 = inverse_scale(q1_r)
    wait_all(recv_sem, 3, dl_r)
    change = unfold(sum_slots(dl_r))
    whole = dot(weigh(predicted - 0.1 * (change * inverse1)), kd[...])
    second = reduce_gradient(5, whole, g2_s, g2_r, lambda: None)
    send_squares(6, second, q2_s, q2_r)
    velocity = first * inverse1
    base = (start - 0.1 * velocity) - 0.1 * (0.9 * velocity)
    wait_all(recv_sem, 6, q2_r)
    out_ref[...] = base - 0.1 * (second * inverse_scale(q2_r))

    for phase, ref in enumerate((data_r, tab_r, g1_r, dl_r, q1_r, g2_r, q2_r)):
        wait_all(send_sem, phase, ref)


def on_device(source, receiver, source_index, receiver_index, observed, noise, huber, start):
    cells = start.shape[0]
    n_data = source_index.shape[0]
    held = [
        pltpu.VMEM((source.shape[0] * COMP, cells), BF16),
        pltpu.VMEM((receiver.shape[0] * COMP, cells), BF16),
        pltpu.VMEM((1, n_data), jnp.int32),
        pltpu.VMEM((1, n_data), jnp.int32),
        pltpu.VMEM((1, n_data), F32),
        pltpu.VMEM((REAL, n_data), jnp.int32),
        pltpu.SMEM((REAL,), jnp.int32),
        pltpu.VMEM((cells // 128, 128), F32),
    ]

    def pair(shape, dtype):
        return [pltpu.VMEM(shape, dtype), pltpu.VMEM((GROUP,) + shape, dtype)]

    return pl.pallas_call(
        functools.partial(body, cells * GROUP),
        out_shape=pltpu.VMEM((REAL, cells), F32),
        in_specs=[pl.BlockSpec(memory_space=pltpu.HBM)] * 8,
        out_specs=pl.BlockSpec(memory_space=pltpu.VMEM),
        scratch_shapes=held
        + [
            pltpu.VMEM((COMP, SOURCES, cells), F32),
            pltpu.VMEM((RECEIVERS, COMP, cells), F32),
            pltpu.VMEM((RECEIVERS, SOURCES, cells), BF16),
            pltpu.VMEM((n_data, cells), BF16),
            pltpu.VMEM((n_data, RECEIVERS * SOURCES), BF16),
            pltpu.VMEM((4, 16, 128), F32),
            pltpu.VMEM((GROUP, 16, 128), F32),
        ]
        + pair((2, 8, 128), F32)
        + pair((16, cells // 2), BF16)
        + pair((16, n_data // 2), BF16)
        + pair((1, 128), F32)
        + pair((16, cells // 2), BF16)
        + pair((1, 128), F32)
        + [
            pltpu.SemaphoreType.DMA((7,)),
            pltpu.SemaphoreType.DMA((7,)),
            pltpu.SemaphoreType.DMA((8,)),
        ],
        compiler_params=pltpu.CompilerParams(collective_id=0, has_side_effects=True),
    )(
        source.reshape(-1, cells),
        receiver.reshape(-1, cells),
        source_index.reshape(1, n_data),
        receiver_index.reshape(1, n_data),
        observed.reshape(1, n_data),
        noise,
        huber,
        start.reshape(-1, 128),
    )


def solution(mesh):
    placed = (
        P(None, None, "cells"),
        P("dp", None, "cells"),
        P("dp"),
        P("dp"),
        P("dp"),
        P(None, "dp"),
        P(),
        P("cells"),
    )
    return jax.shard_map(
        on_device, mesh=mesh, in_specs=placed, out_specs=P(None, "cells"), check_vma=False
    )
```

```python
import functools
import math

import jax
import jax.numpy as jnp
from jax import lax
from jax.experimental import pallas as pl
from jax.experimental.pallas import tpu as pltpu
from jax.sharding import PartitionSpec as P

F32 = jnp.float32
BF16 = jnp.bfloat16
GROUP = 16
COMP = 8
REAL = 8
SOURCES = 48
RECEIVERS = 32
MESH = pl.DeviceIdType.MESH


def hops(step, ring):
    return min(step, ring - step)


CELLS_ORDER = sorted(
    ((step, flip) for step in range(8) for flip in range(2) if step or flip),
    key=lambda p: -(hops(p[0], 8) + 2 * p[1]),
)
DP_ORDER = sorted(
    ((y, x, core) for y in range(4) for x in range(2) for core in range(2) if y or x or core),
    key=lambda p: -((0, 1, 2, 1)[p[0]] + p[1] + 0.1 * p[2]),
)
ORDERS = {"cells": CELLS_ORDER, "dp": DP_ORDER}


def iota(shape, axis):
    return lax.broadcasted_iota(jnp.int32, shape, axis)


def dot(a, b):
    return jnp.dot(a, b, preferred_element_type=F32)


def dot_nt(a, b):
    return lax.dot_general(a, b, (((1,), (1,)), ((), ())), preferred_element_type=F32)


def split_halves(table):
    high = table.astype(BF16).astype(F32)
    return jnp.where(iota(table.shape, 1) < 64, high, table - high).astype(BF16)


def body(
    cells_total,
    *refs,
):
    given, out_ref, held, refs = refs[:8], refs[8], refs[9:17], refs[17:]
    src_ref, rec_ref, sidx_ref, ridx_ref, obs_ref, noise_ref, huber_ref, start_ref = held
    sf, rk, ka, kd, oh, data_s, data_r, tab_s, tab_r, g1_s, g1_r, dl_s, dl_r, q1_s, q1_r = refs[:15]
    g2_s, g2_r, q2_s, q2_r, send_sem, recv_sem, load_sem = refs[15:]
    me_dp = lax.axis_index("dp")
    me_cells = lax.axis_index("cells")
    cells = src_ref.shape[1]
    n_data = sidx_ref.shape[1]
    scale = 0.2 / math.sqrt(COMP * cells_total)

    def flipped(value, bit, flip):
        return lax.rem(value // bit + flip, 2) * bit

    def peer(axis, pattern):
        if axis == "cells":
            step, flip = pattern
            return 2 * lax.rem(me_cells // 2 + step, 8) + flipped(me_cells, 1, flip)
        y, x, core = pattern
        me = me_dp
        return (
            flipped(me, 8, y // 2) + flipped(me, 4, y % 2) + flipped(me, 2, x) + flipped(me, 1, core)
        )

    barrier = pltpu.get_barrier_semaphore()

    def greet(axis, patterns):
        for pattern in patterns:
            pl.semaphore_signal(
                barrier, inc=1, device_id={axis: peer(axis, pattern)}, device_id_type=MESH
            )

    greet("cells", CELLS_ORDER[:8])
    loads = [
        pltpu.make_async_copy(a, b, load_sem.at[n]) for n, (a, b) in enumerate(zip(given, held))
    ]
    for n in (3, 2, 4, 5, 1, 7, 0, 6):
        loads[n].start()
    greet("cells", CELLS_ORDER[8:])
    greet("dp", DP_ORDER)

    def send_all(axis, phase, src_of, arrived):
        mine = me_cells if axis == "cells" else me_dp
        for pattern in ORDERS[axis]:
            other = peer(axis, pattern)
            pltpu.make_async_remote_copy(
                src_ref=src_of(other),
                dst_ref=arrived.at[mine],
                send_sem=send_sem.at[phase],
                recv_sem=recv_sem.at[phase],
                device_id={axis: other},
                device_id_type=MESH,
            ).start()

    def fold(x):
        half = x.shape[1] // 2
        return jnp.concatenate([x[:, :half], x[:, half:]], axis=0)

    def unfold(x):
        half = x.shape[0] // 2
        return jnp.concatenate([x[:half], x[half:]], axis=1)

    def sum_slots(arrived):
        parts = [arrived[o].astype(F32) for o in range(GROUP)]
        while len(parts) > 1:
            parts = [a + b for a, b in zip(parts[::2], parts[1::2])]
        return parts[0]

    def wait_all(sem, phase, ref):
        part = ref.at[pl.ds(0, GROUP - 1)]
        pltpu.make_async_copy(part, part, sem.at[phase]).wait()

    for n in range(2, 7):
        loads[n].wait()
    owner = ridx_ref[...] // 32
    local = ridx_ref[...] % 32
    member = (iota((16, n_data), 0) == owner).astype(F32)
    before = (iota((n_data, n_data), 0) < iota((n_data, n_data), 1)).astype(F32).astype(BF16)
    rank = jnp.sum(member * dot(member.astype(BF16), before), axis=0, keepdims=True)
    place = (128 * (owner // 4) + 32 * ((owner + me_dp) % 4)).astype(F32) + rank
    move = (iota((n_data, n_data), 0).astype(F32) == place).astype(F32).astype(BF16)
    shifted = obs_ref[...] + noise_ref[...].astype(F32) / 4096.0
    high = shifted.astype(BF16).astype(F32)
    middle = (shifted - high).astype(BF16).astype(F32)
    low = shifted - high - middle
    row8 = iota((8, n_data), 0)
    index_rows = jnp.where(
        row8 == 0,
        sidx_ref[...].astype(F32),
        jnp.where(row8 == 1, local.astype(F32), 0.0),
    )
    moved = dot_nt(jnp.concatenate([high, middle, low, index_rows], axis=0).astype(BF16), move)
    shifted = moved[0:8] + moved[8:16] + moved[16:24]
    for t in range(4):
        data_s[t, 0:8, :] = shifted[:, 128 * t : 128 * t + 128]
        data_s[t, 8:16, :] = moved[24:32, 128 * t : 128 * t + 128]

    for n in (1, 7):
        loads[n].wait()
    start = jnp.concatenate([start_ref[n : n + 1, :] for n in range(cells // 128)], axis=1)
    exact = rec_ref[...].astype(F32) * start.astype(BF16).astype(F32)
    high = exact.astype(BF16)
    low = (exact - high.astype(F32)).astype(BF16)
    loads[0].wait()
    cross = dot_nt(high, src_ref[...]) + dot_nt(low, src_ref[...])
    shape = (COMP, SOURCES * COMP)
    odd = iota(shape, 0) % 2
    keep = jnp.where(iota(shape, 1) % COMP == iota(shape, 0), 1.0 - 2.0 * odd.astype(F32), 0.0)
    table = jnp.concatenate(
        [
            jnp.sum(cross[COMP * r : COMP * r + COMP] * keep, axis=0, keepdims=True)
            for r in range(RECEIVERS)
        ],
        axis=0,
    )
    high = table.astype(BF16)
    low = (table - high.astype(F32)).astype(BF16)
    shape = (SOURCES * COMP, 128)
    group = (iota(shape, 0) // COMP == iota(shape, 1) % 64).astype(F32).astype(BF16)
    table = dot(jnp.concatenate([high, low], axis=0), group)
    table = (table[:RECEIVERS] + table[RECEIVERS:]) * scale
    left = iota((8, 128), 1) < 64
    tab_s[0] = jnp.where(left, table[0:8], table[8:16])
    tab_s[1] = jnp.where(left, table[16:24], table[24:32])

    pl.semaphore_wait(barrier, 2 * (GROUP - 1))
    send_all("dp", 0, lambda o: data_s.at[o // 4], data_r)
    send_all("cells", 1, lambda o: tab_s, tab_r)

    pick = (
        (iota((128, 128), 0) % 16) * COMP + iota((128, 128), 0) // 16 == iota((128, 128), 1)
    ).astype(F32).astype(BF16)
    for chunk in range(3):
        rows = dot(pick, src_ref[128 * chunk : 128 * chunk + 128, :])
        for c in range(COMP):
            sf[c, 16 * chunk : 16 * chunk + 16, :] = rows[16 * c : 16 * c + 16, :]

    signs = jnp.where(iota((COMP, cells), 0) % 2 == 0, scale, -scale)
    for r in range(RECEIVERS):
        rk[r] = rec_ref[COMP * r : COMP * r + COMP, :].astype(F32) * signs

    def form(r, carry):
        for n in range(cells // 128):
            lanes = slice(128 * n, 128 * n + 128)
            factors = rk[r, :, lanes]
            rows = sf[0, :, lanes] * factors[0:1]
            for c in range(1, COMP):
                rows = rows + sf[c, :, lanes] * factors[c : c + 1]
            ka[r, :, lanes] = rows.astype(BF16)
        return carry

    lax.fori_loop(0, RECEIVERS, form, 0)

    data_r[me_dp] = data_s[me_dp // 4]
    tab_r[me_cells] = tab_s[...]
    wait_all(recv_sem, 0, data_r)
    quarter = iota((16, 128), 1) // 32
    tiles = []
    for t in range(4):
        tile = data_r[4 * t]
        for sender in range(4 * t + 1, 4 * t + 4):
            tile = jnp.where(quarter == lax.rem(me_dp + sender, 4), data_r[sender], tile)
        tiles.append(tile)
    data = jnp.concatenate(tiles, axis=1)
    shifted = data[0:8]
    column = jnp.transpose(data[8:16])
    code = column[:, 1:2] * SOURCES + column[:, 0:1]
    pairs = RECEIVERS * SOURCES
    oh[...] = (iota((n_data, pairs), 1).astype(F32) == code).astype(F32).astype(BF16)
    source = data[8:9].astype(jnp.int32)
    receiver = data[9:10].astype(jnp.int32)
    is_source = (iota((128, n_data), 0) % 64 == source).astype(F32).astype(BF16)
    is_receiver = (iota((32, n_data), 0) == receiver).astype(F32)
    limit = jnp.zeros((REAL, n_data), F32)
    for k in range(REAL):
        limit = jnp.where(row8 == k, huber_ref[k].astype(F32) / 16.0, limit)

    wait_all(recv_sem, 1, tab_r)
    packed = sum_slots(tab_r)
    rows = []
    for t in range(2):
        here = packed[t]
        turned = pltpu.roll(here, 64, 1)
        rows.append(jnp.where(left, here, turned))
        rows.append(jnp.where(left, turned, here))
    spread = dot(split_halves(jnp.concatenate(rows, axis=0)), is_source)
    predicted = jnp.sum(spread * is_receiver, axis=0, keepdims=True)

    def two_parts(x):
        high = x.astype(BF16).astype(F32)
        return jnp.concatenate([high, x - high], axis=0).astype(BF16)

    def weigh(predicted):
        return jnp.clip(predicted - shifted, -limit, limit).astype(BF16)

    def reduce_gradient(phase, whole, part, arrived, meanwhile):
        part[...] = fold(whole).astype(BF16)
        send_all("dp", phase, lambda o: part, arrived)
        arrived[me_dp] = part[...]
        meanwhile()
        wait_all(recv_sem, phase, arrived)
        return unfold(sum_slots(arrived))

    def send_squares(phase, whole, part, arrived):
        squares = jnp.sum(whole * whole, axis=1, keepdims=True)
        diagonal = iota((REAL, 128), 0) == iota((REAL, 128), 1)
        part[...] = jnp.sum(jnp.where(diagonal, squares, 0.0), axis=0, keepdims=True)
        send_all("cells", phase, lambda o: part, arrived)
        arrived[me_cells] = part[...]

    def inverse_scale(arrived):
        total = sum_slots(arrived)
        diagonal = iota((REAL, 128), 0) == iota((REAL, 128), 1)
        column = jnp.sum(jnp.where(diagonal, total, 0.0), axis=1, keepdims=True)
        return 1.0 / jnp.sqrt(column / cells_total + 1e-06)

    def pick_rows():
        kd[...] = dot(oh[...], ka[...].reshape(pairs, cells)).astype(BF16)

    both = dot(two_parts(dot(weigh(predicted), oh[...])), ka[...].reshape(pairs, cells))
    first = reduce_gradient(2, both[:REAL] + both[REAL:], g1_s, g1_r, pick_rows)
    send_squares(4, first, q1_s, q1_r)

    both = dot_nt(two_parts(first), kd[...])
    change = both[:REAL] + both[REAL:]
    dl_s[...] = fold(change).astype(BF16)
    send_all("cells", 3, lambda o: dl_s, dl_r)
    dl_r[me_cells] = dl_s[...]
    wait_all(recv_sem, 4, q1_r)
    inverse1 = inverse_scale(q1_r)
    wait_all(recv_sem, 3, dl_r)
    change = unfold(sum_slots(dl_r))
    whole = dot(weigh(predicted - 0.1 * (change * inverse1)), kd[...])
    second = reduce_gradient(5, whole, g2_s, g2_r, lambda: None)
    send_squares(6, second, q2_s, q2_r)
    velocity = first * inverse1
    base = (start - 0.1 * velocity) - 0.1 * (0.9 * velocity)
    wait_all(recv_sem, 6, q2_r)
    out_ref[...] = base - 0.1 * (second * inverse_scale(q2_r))

    for phase, ref in enumerate((data_r, tab_r, g1_r, dl_r, q1_r, g2_r, q2_r)):
        wait_all(send_sem, phase, ref)


def on_device(source, receiver, source_index, receiver_index, observed, noise, huber, start):
    cells = start.shape[0]
    n_data = source_index.shape[0]
    held = [
        pltpu.VMEM((source.shape[0] * COMP, cells), BF16),
        pltpu.VMEM((receiver.shape[0] * COMP, cells), BF16),
        pltpu.VMEM((1, n_data), jnp.int32),
        pltpu.VMEM((1, n_data), jnp.int32),
        pltpu.VMEM((1, n_data), F32),
        pltpu.VMEM((REAL, n_data), jnp.int32),
        pltpu.SMEM((REAL,), jnp.int32),
        pltpu.VMEM((cells // 128, 128), F32),
    ]

    def pair(shape, dtype):
        return [pltpu.VMEM(shape, dtype), pltpu.VMEM((GROUP,) + shape, dtype)]

    return pl.pallas_call(
        functools.partial(body, cells * GROUP),
        out_shape=pltpu.VMEM((REAL, cells), F32),
        in_specs=[pl.BlockSpec(memory_space=pltpu.HBM)] * 8,
        out_specs=pl.BlockSpec(memory_space=pltpu.VMEM),
        scratch_shapes=held
        + [
            pltpu.VMEM((COMP, SOURCES, cells), F32),
            pltpu.VMEM((RECEIVERS, COMP, cells), F32),
            pltpu.VMEM((RECEIVERS, SOURCES, cells), BF16),
            pltpu.VMEM((n_data, cells), BF16),
            pltpu.VMEM((n_data, RECEIVERS * SOURCES), BF16),
            pltpu.VMEM((4, 16, 128), F32),
            pltpu.VMEM((GROUP, 16, 128), F32),
        ]
        + pair((2, 8, 128), F32)
        + pair((16, cells // 2), BF16)
        + pair((16, n_data // 2), BF16)
        + pair((1, 128), F32)
        + pair((16, cells // 2), BF16)
        + pair((1, 128), F32)
        + [
            pltpu.SemaphoreType.DMA((7,)),
            pltpu.SemaphoreType.DMA((7,)),
            pltpu.SemaphoreType.DMA((8,)),
        ],
        compiler_params=pltpu.CompilerParams(collective_id=0, has_side_effects=True),
    )(
        source.reshape(-1, cells),
        receiver.reshape(-1, cells),
        source_index.reshape(1, n_data),
        receiver_index.reshape(1, n_data),
        observed.reshape(1, n_data),
        noise,
        huber,
        start.reshape(-1, 128),
    )


def solution(mesh):
    placed = (
        P(None, None, "cells"),
        P("dp", None, "cells"),
        P("dp"),
        P("dp"),
        P("dp"),
        P(None, "dp"),
        P(),
        P("cells"),
    )
    return jax.shard_map(
        on_device, mesh=mesh, in_specs=placed, out_specs=P(None, "cells"), check_vma=False
    )
```

```python
import functools
import math

import jax
import jax.numpy as jnp
from jax import lax
from jax.experimental import pallas as pl
from jax.experimental.pallas import tpu as pltpu
from jax.sharding import PartitionSpec as P

F32 = jnp.float32
BF16 = jnp.bfloat16
GROUP = 16
COMP = 8
REAL = 8
SOURCES = 48
RECEIVERS = 32
MESH = pl.DeviceIdType.MESH


def hops(step, ring):
    return min(step, ring - step)


CELLS_ORDER = sorted(
    ((step, flip) for step in range(8) for flip in range(2) if step or flip),
    key=lambda p: -(hops(p[0], 8) + 2 * p[1]),
)
DP_ORDER = sorted(
    ((y, x, core) for y in range(4) for x in range(2) for core in range(2) if y or x or core),
    key=lambda p: -((0, 1, 2, 1)[p[0]] + p[1] + 0.1 * p[2]),
)
ORDERS = {"cells": CELLS_ORDER, "dp": DP_ORDER}


def iota(shape, axis):
    return lax.broadcasted_iota(jnp.int32, shape, axis)


def dot(a, b):
    return jnp.dot(a, b, preferred_element_type=F32)


def dot_nt(a, b):
    return lax.dot_general(a, b, (((1,), (1,)), ((), ())), preferred_element_type=F32)


def split_halves(table):
    high = table.astype(BF16).astype(F32)
    return jnp.where(iota(table.shape, 1) < 64, high, table - high).astype(BF16)


def body(
    cells_total,
    *refs,
):
    given, out_ref, held, refs = refs[:8], refs[8], refs[9:17], refs[17:]
    src_ref, rec_ref, sidx_ref, ridx_ref, obs_ref, noise_ref, huber_ref, start_ref = held
    sf, rk, ka, kd, oh, data_s, data_r, tab_s, tab_r, g1_s, g1_r, dl_s, dl_r, q1_s, q1_r = refs[:15]
    g2_s, g2_r, q2_s, q2_r, send_sem, recv_sem, load_sem = refs[15:]
    me_dp = lax.axis_index("dp")
    me_cells = lax.axis_index("cells")
    cells = src_ref.shape[1]
    n_data = sidx_ref.shape[1]
    scale = 0.2 / math.sqrt(COMP * cells_total)

    def flipped(value, bit, flip):
        return lax.rem(value // bit + flip, 2) * bit

    def peer(axis, pattern):
        if axis == "cells":
            step, flip = pattern
            return 2 * lax.rem(me_cells // 2 + step, 8) + flipped(me_cells, 1, flip)
        y, x, core = pattern
        me = me_dp
        return (
            flipped(me, 8, y // 2) + flipped(me, 4, y % 2) + flipped(me, 2, x) + flipped(me, 1, core)
        )

    barrier = pltpu.get_barrier_semaphore()

    def greet(axis, patterns):
        for pattern in patterns:
            pl.semaphore_signal(
                barrier, inc=1, device_id={axis: peer(axis, pattern)}, device_id_type=MESH
            )

    greet("cells", CELLS_ORDER[:8])
    loads = [
        pltpu.make_async_copy(a, b, load_sem.at[n]) for n, (a, b) in enumerate(zip(given, held))
    ]
    for n in (3, 2, 4, 5, 1, 7, 0, 6):
        loads[n].start()
    greet("cells", CELLS_ORDER[8:])
    greet("dp", DP_ORDER)

    def send_all(axis, phase, src_of, arrived):
        mine = me_cells if axis == "cells" else me_dp
        for pattern in ORDERS[axis]:
            other = peer(axis, pattern)
            pltpu.make_async_remote_copy(
                src_ref=src_of(other),
                dst_ref=arrived.at[mine],
                send_sem=send_sem.at[phase],
                recv_sem=recv_sem.at[phase],
                device_id={axis: other},
                device_id_type=MESH,
            ).start()

    def fold(x):
        half = x.shape[1] // 2
        return jnp.concatenate([x[:, :half], x[:, half:]], axis=0)

    def unfold(x):
        half = x.shape[0] // 2
        return jnp.concatenate([x[:half], x[half:]], axis=1)

    def sum_slots(arrived):
        parts = [arrived[o].astype(F32) for o in range(GROUP)]
        while len(parts) > 1:
            parts = [a + b for a, b in zip(parts[::2], parts[1::2])]
        return parts[0]

    def wait_all(sem, phase, ref):
        part = ref.at[pl.ds(0, GROUP - 1)]
        pltpu.make_async_copy(part, part, sem.at[phase]).wait()

    for n in range(2, 7):
        loads[n].wait()
    owner = ridx_ref[...] // 32
    local = ridx_ref[...] % 32
    member = (iota((16, n_data), 0) == owner).astype(F32)
    before = (iota((n_data, n_data), 0) < iota((n_data, n_data), 1)).astype(F32).astype(BF16)
    rank = jnp.sum(member * dot(member.astype(BF16), before), axis=0, keepdims=True)
    place = (128 * (owner // 4) + 32 * ((owner + me_dp) % 4)).astype(F32) + rank
    move = (iota((n_data, n_data), 0).astype(F32) == place).astype(F32).astype(BF16)
    shifted = obs_ref[...] + noise_ref[...].astype(F32) / 4096.0
    high = shifted.astype(BF16).astype(F32)
    middle = (shifted - high).astype(BF16).astype(F32)
    low = shifted - high - middle
    row8 = iota((8, n_data), 0)
    index_rows = jnp.where(
        row8 == 0,
        sidx_ref[...].astype(F32),
        jnp.where(row8 == 1, local.astype(F32), 0.0),
    )
    moved = dot_nt(jnp.concatenate([high, middle, low, index_rows], axis=0).astype(BF16), move)
    shifted = moved[0:8] + moved[8:16] + moved[16:24]
    quarter = iota((8, 128), 1) // 32
    for t in range(4):
        lanes = slice(128 * t, 128 * t + 128)
        beside = pltpu.roll(moved[24:32, lanes], 32, 1)
        for o in range(4 * t, 4 * t + 4):
            data_s[o] = jnp.where(quarter == lax.rem(me_dp + o, 4), shifted[:, lanes], beside)

    for n in (1, 7):
        loads[n].wait()
    start = jnp.concatenate([start_ref[n : n + 1, :] for n in range(cells // 128)], axis=1)
    exact = rec_ref[...].astype(F32) * start.astype(BF16).astype(F32)
    high = exact.astype(BF16)
    low = (exact - high.astype(F32)).astype(BF16)
    loads[0].wait()
    cross = dot_nt(high, src_ref[...]) + dot_nt(low, src_ref[...])
    shape = (COMP, SOURCES * COMP)
    odd = iota(shape, 0) % 2
    keep = jnp.where(iota(shape, 1) % COMP == iota(shape, 0), 1.0 - 2.0 * odd.astype(F32), 0.0)
    table = jnp.concatenate(
        [
            jnp.sum(cross[COMP * r : COMP * r + COMP] * keep, axis=0, keepdims=True)
            for r in range(RECEIVERS)
        ],
        axis=0,
    )
    high = table.astype(BF16)
    low = (table - high.astype(F32)).astype(BF16)
    shape = (SOURCES * COMP, 128)
    group = (iota(shape, 0) // COMP == iota(shape, 1) % 64).astype(F32).astype(BF16)
    table = dot(jnp.concatenate([high, low], axis=0), group)
    table = (table[:RECEIVERS] + table[RECEIVERS:]) * scale
    left = iota((8, 128), 1) < 64
    tab_s[...] = jnp.concatenate(
        [jnp.where(left, table[0:8], table[8:16]), jnp.where(left, table[16:24], table[24:32])], axis=0
    ).astype(BF16)

    pl.semaphore_wait(barrier, 2 * (GROUP - 1))
    send_all("cells", 1, lambda o: tab_s, tab_r)
    send_all("dp", 0, lambda o: data_s.at[o], data_r)

    pick = (
        (iota((128, 128), 0) % 16) * COMP + iota((128, 128), 0) // 16 == iota((128, 128), 1)
    ).astype(F32).astype(BF16)
    for chunk in range(3):
        rows = dot(pick, src_ref[128 * chunk : 128 * chunk + 128, :])
        for c in range(COMP):
            sf[c, 16 * chunk : 16 * chunk + 16, :] = rows[16 * c : 16 * c + 16, :]

    signs = jnp.where(iota((COMP, cells), 0) % 2 == 0, scale, -scale)
    for r in range(RECEIVERS):
        rk[r] = rec_ref[COMP * r : COMP * r + COMP, :].astype(F32) * signs

    def form(r, carry):
        for n in range(cells // 128):
            lanes = slice(128 * n, 128 * n + 128)
            factors = rk[r, :, lanes]
            rows = sf[0, :, lanes] * factors[0:1]
            for c in range(1, COMP):
                rows = rows + sf[c, :, lanes] * factors[c : c + 1]
            ka[r, :, lanes] = rows.astype(BF16)
        return carry

    lax.fori_loop(0, RECEIVERS, form, 0)

    data_r[me_dp] = data_s[me_dp]
    tab_r[me_cells] = tab_s[...]
    wait_all(recv_sem, 0, data_r)
    values, indices = [], []
    for t in range(4):
        tile = beside = data_r[4 * t]
        for sender in range(4 * t + 1, 4 * t + 4):
            here = data_r[sender]
            tile = jnp.where(quarter == lax.rem(me_dp + sender, 4), here, tile)
            beside = jnp.where(quarter == lax.rem(me_dp + sender + 1, 4), here, beside)
        values.append(tile)
        indices.append(pltpu.roll(beside, 96, 1))
    shifted = jnp.concatenate(values, axis=1)
    indices = jnp.concatenate(indices, axis=1)
    column = jnp.transpose(indices)
    code = column[:, 1:2] * SOURCES + column[:, 0:1]
    pairs = RECEIVERS * SOURCES
    oh[...] = (iota((n_data, pairs), 1).astype(F32) == code).astype(F32).astype(BF16)
    source = indices[0:1].astype(jnp.int32)
    receiver = indices[1:2].astype(jnp.int32)
    is_source = (iota((128, n_data), 0) % 64 == source).astype(F32).astype(BF16)
    is_receiver = (iota((32, n_data), 0) == receiver).astype(F32)
    limit = jnp.zeros((REAL, n_data), F32)
    for k in range(REAL):
        limit = jnp.where(row8 == k, huber_ref[k].astype(F32) / 16.0, limit)

    wait_all(recv_sem, 1, tab_r)
    packed = sum_slots(tab_r)
    rows = []
    for t in range(2):
        here = packed[8 * t : 8 * t + 8]
        turned = pltpu.roll(here, 64, 1)
        rows.append(jnp.where(left, here, turned))
        rows.append(jnp.where(left, turned, here))
    spread = dot(split_halves(jnp.concatenate(rows, axis=0)), is_source)
    predicted = jnp.sum(spread * is_receiver, axis=0, keepdims=True)

    def two_parts(x):
        high = x.astype(BF16).astype(F32)
        return jnp.concatenate([high, x - high], axis=0).astype(BF16)

    def weigh(predicted):
        return jnp.clip(predicted - shifted, -limit, limit).astype(BF16)

    def reduce_gradient(phase, whole, part, arrived, meanwhile):
        part[...] = fold(whole).astype(BF16)
        send_all("dp", phase, lambda o: part, arrived)
        arrived[me_dp] = part[...]
        meanwhile()
        wait_all(recv_sem, phase, arrived)
        return unfold(sum_slots(arrived))

    def send_squares(phase, whole, part, arrived):
        squares = jnp.sum(whole * whole, axis=1, keepdims=True)
        diagonal = iota((REAL, 128), 0) == iota((REAL, 128), 1)
        part[...] = jnp.sum(jnp.where(diagonal, squares, 0.0), axis=0, keepdims=True)
        send_all("cells", phase, lambda o: part, arrived)
        arrived[me_cells] = part[...]

    def inverse_scale(arrived):
        total = sum_slots(arrived)
        diagonal = iota((REAL, 128), 0) == iota((REAL, 128), 1)
        column = jnp.sum(jnp.where(diagonal, total, 0.0), axis=1, keepdims=True)
        return 1.0 / jnp.sqrt(column / cells_total + 1e-06)

    def pick_rows():
        kd[...] = dot(oh[...], ka[...].reshape(pairs, cells)).astype(BF16)

    both = dot(two_parts(dot(weigh(predicted), oh[...])), ka[...].reshape(pairs, cells))
    first = reduce_gradient(2, both[:REAL] + both[REAL:], g1_s, g1_r, pick_rows)
    send_squares(4, first, q1_s, q1_r)

    both = dot_nt(two_parts(first), kd[...])
    change = both[:REAL] + both[REAL:]
    dl_s[...] = fold(change).astype(BF16)
    send_all("cells", 3, lambda o: dl_s, dl_r)
    dl_r[me_cells] = dl_s[...]
    wait_all(recv_sem, 4, q1_r)
    inverse1 = inverse_scale(q1_r)
    wait_all(recv_sem, 3, dl_r)
    change = unfold(sum_slots(dl_r))
    whole = dot(weigh(predicted - 0.1 * (change * inverse1)), kd[...])
    second = reduce_gradient(5, whole, g2_s, g2_r, lambda: None)
    send_squares(6, second, q2_s, q2_r)
    velocity = first * inverse1
    base = (start - 0.1 * velocity) - 0.1 * (0.9 * velocity)
    wait_all(recv_sem, 6, q2_r)
    out_ref[...] = base - 0.1 * (second * inverse_scale(q2_r))

    for phase, ref in enumerate((data_r, tab_r, g1_r, dl_r, q1_r, g2_r, q2_r)):
        wait_all(send_sem, phase, ref)


def on_device(source, receiver, source_index, receiver_index, observed, noise, huber, start):
    cells = start.shape[0]
    n_data = source_index.shape[0]
    held = [
        pltpu.VMEM((source.shape[0] * COMP, cells), BF16),
        pltpu.VMEM((receiver.shape[0] * COMP, cells), BF16),
        pltpu.VMEM((1, n_data), jnp.int32),
        pltpu.VMEM((1, n_data), jnp.int32),
        pltpu.VMEM((1, n_data), F32),
        pltpu.VMEM((REAL, n_data), jnp.int32),
        pltpu.SMEM((REAL,), jnp.int32),
        pltpu.VMEM((cells // 128, 128), F32),
    ]

    def pair(shape, dtype):
        return [pltpu.VMEM(shape, dtype), pltpu.VMEM((GROUP,) + shape, dtype)]

    return pl.pallas_call(
        functools.partial(body, cells * GROUP),
        out_shape=pltpu.VMEM((REAL, cells), F32),
        in_specs=[pl.BlockSpec(memory_space=pltpu.HBM)] * 8,
        out_specs=pl.BlockSpec(memory_space=pltpu.VMEM),
        scratch_shapes=held
        + [
            pltpu.VMEM((COMP, SOURCES, cells), F32),
            pltpu.VMEM((RECEIVERS, COMP, cells), F32),
            pltpu.VMEM((RECEIVERS, SOURCES, cells), BF16),
            pltpu.VMEM((n_data, cells), BF16),
            pltpu.VMEM((n_data, RECEIVERS * SOURCES), BF16),
            pltpu.VMEM((GROUP, 8, 128), F32),
            pltpu.VMEM((GROUP, 8, 128), F32),
        ]
        + pair((16, 128), BF16)
        + pair((16, cells // 2), BF16)
        + pair((16, n_data // 2), BF16)
        + pair((1, 128), F32)
        + pair((16, cells // 2), BF16)
        + pair((1, 128), F32)
        + [
            pltpu.SemaphoreType.DMA((7,)),
            pltpu.SemaphoreType.DMA((7,)),
            pltpu.SemaphoreType.DMA((8,)),
        ],
        compiler_params=pltpu.CompilerParams(collective_id=0, has_side_effects=True),
    )(
        source.reshape(-1, cells),
        receiver.reshape(-1, cells),
        source_index.reshape(1, n_data),
        receiver_index.reshape(1, n_data),
        observed.reshape(1, n_data),
        noise,
        huber,
        start.reshape(-1, 128),
    )


def solution(mesh):
    placed = (
        P(None, None, "cells"),
        P("dp", None, "cells"),
        P("dp"),
        P("dp"),
        P("dp"),
        P(None, "dp"),
        P(),
        P("cells"),
    )
    return jax.shard_map(
        on_device, mesh=mesh, in_specs=placed, out_specs=P(None, "cells"), check_vma=False
    )
```

```python
import functools
import math

import jax
import jax.numpy as jnp
from jax import lax
from jax.experimental import pallas as pl
from jax.experimental.pallas import tpu as pltpu
from jax.sharding import PartitionSpec as P

F32 = jnp.float32
BF16 = jnp.bfloat16
GROUP = 16
COMP = 8
REAL = 8
SOURCES = 48
RECEIVERS = 32
LOGICAL = pl.DeviceIdType.LOGICAL


def hops(step, ring):
    return min(step, ring - step)


CELLS_ORDER = sorted(
    ((step, flip) for step in range(8) for flip in range(2) if step or flip),
    key=lambda p: -(hops(p[0], 8) + 2 * p[1]),
)
DP_ORDER = sorted(
    ((y, x, core) for y in range(4) for x in range(2) for core in range(2) if y or x or core),
    key=lambda p: -((0, 1, 2, 1)[p[0]] + p[1] + 0.1 * p[2]),
)


def iota(shape, axis):
    return lax.broadcasted_iota(jnp.int32, shape, axis)


def dot(a, b):
    return jnp.dot(a, b, preferred_element_type=F32)


def dot_nt(a, b):
    return lax.dot_general(a, b, (((1,), (1,)), ((), ())), preferred_element_type=F32)


def split_halves(table):
    high = table.astype(BF16).astype(F32)
    return jnp.where(iota(table.shape, 1) < 64, high, table - high).astype(BF16)


def body(
    cells_total,
    *refs,
):
    given, out_ref, held, refs = refs[:8], refs[8], refs[9:17], refs[17:]
    src_ref, rec_ref, sidx_ref, ridx_ref, obs_ref, noise_ref, huber_ref, start_ref = held
    sf, rk, ka, kd, oh, data_s, data_r, tab_s, tab_r, g1_s, g1_r, dl_s, dl_r, q1_s, q1_r = refs[:15]
    g2_s, g2_r, q2_s, q2_r, send_sem, recv_sem, load_sem = refs[15:]
    me_dp = lax.axis_index("dp")
    me_cells = lax.axis_index("cells")
    cells = src_ref.shape[1]
    n_data = sidx_ref.shape[1]
    scale = 0.2 / math.sqrt(COMP * cells_total)

    def flipped(value, bit, flip):
        return lax.rem(value // bit + flip, 2) * bit

    def peer(axis, pattern):
        if axis == "cells":
            step, flip = pattern
            return 2 * lax.rem(me_cells // 2 + step, 8) + flipped(me_cells, 1, flip)
        y, x, core = pattern
        me = me_dp
        return (
            flipped(me, 8, y // 2) + flipped(me, 4, y % 2) + flipped(me, 2, x) + flipped(me, 1, core)
        )

    peers = {
        "cells": [(peer("cells", p), me_dp * GROUP + peer("cells", p)) for p in CELLS_ORDER],
        "dp": [(peer("dp", p), peer("dp", p) * GROUP + me_cells) for p in DP_ORDER],
    }

    barrier = pltpu.get_barrier_semaphore()

    def greet(axis, patterns):
        for _, device in patterns:
            pl.semaphore_signal(barrier, inc=1, device_id=device, device_id_type=LOGICAL)

    greet("cells", peers["cells"][:8])
    loads = [
        pltpu.make_async_copy(a, b, load_sem.at[n]) for n, (a, b) in enumerate(zip(given, held))
    ]
    for n in (3, 2, 4, 5, 1, 7, 0, 6):
        loads[n].start()
    greet("cells", peers["cells"][8:])
    greet("dp", peers["dp"])

    def send_all(axis, phase, src_of, arrived):
        mine = me_cells if axis == "cells" else me_dp
        for other, device in peers[axis]:
            pltpu.make_async_remote_copy(
                src_ref=src_of(other),
                dst_ref=arrived.at[mine],
                send_sem=send_sem.at[phase],
                recv_sem=recv_sem.at[phase],
                device_id=device,
                device_id_type=LOGICAL,
            ).start()

    def fold(x):
        half = x.shape[1] // 2
        return jnp.concatenate([x[:, :half], x[:, half:]], axis=0)

    def unfold(x):
        half = x.shape[0] // 2
        return jnp.concatenate([x[:half], x[half:]], axis=1)

    def sum_slots(arrived):
        parts = [arrived[o].astype(F32) for o in range(GROUP)]
        while len(parts) > 1:
            parts = [a + b for a, b in zip(parts[::2], parts[1::2])]
        return parts[0]

    def wait_all(sem, phase, ref):
        part = ref.at[pl.ds(0, GROUP - 1)]
        pltpu.make_async_copy(part, part, sem.at[phase]).wait()

    for n in range(2, 7):
        loads[n].wait()
    owner = ridx_ref[...] // 32
    local = ridx_ref[...] % 32
    member = (iota((16, n_data), 0) == owner).astype(F32)
    before = (iota((n_data, n_data), 0) < iota((n_data, n_data), 1)).astype(F32).astype(BF16)
    rank = jnp.sum(member * dot(member.astype(BF16), before), axis=0, keepdims=True)
    place = (128 * (owner // 4) + 32 * ((owner + me_dp) % 4)).astype(F32) + rank
    move = (iota((n_data, n_data), 0).astype(F32) == place).astype(F32).astype(BF16)
    shifted = obs_ref[...] + noise_ref[...].astype(F32) / 4096.0
    high = shifted.astype(BF16).astype(F32)
    middle = (shifted - high).astype(BF16).astype(F32)
    low = shifted - high - middle
    row8 = iota((8, n_data), 0)
    index_rows = jnp.where(
        row8 == 0,
        sidx_ref[...].astype(F32),
        jnp.where(row8 == 1, local.astype(F32), 0.0),
    )
    moved = dot_nt(jnp.concatenate([high, middle, low, index_rows], axis=0).astype(BF16), move)
    shifted = moved[0:8] + moved[8:16] + moved[16:24]
    quarter = iota((8, 128), 1) // 32
    for t in range(4):
        lanes = slice(128 * t, 128 * t + 128)
        beside = pltpu.roll(moved[24:32, lanes], 32, 1)
        for o in range(4 * t, 4 * t + 4):
            data_s[o] = jnp.where(quarter == lax.rem(me_dp + o, 4), shifted[:, lanes], beside)

    for n in (1, 7):
        loads[n].wait()
    start = jnp.concatenate([start_ref[n : n + 1, :] for n in range(cells // 128)], axis=1)
    exact = rec_ref[...].astype(F32) * start.astype(BF16).astype(F32)
    high = exact.astype(BF16)
    low = (exact - high.astype(F32)).astype(BF16)
    loads[0].wait()
    cross = dot_nt(high, src_ref[...]) + dot_nt(low, src_ref[...])
    shape = (COMP, SOURCES * COMP)
    odd = iota(shape, 0) % 2
    keep = jnp.where(iota(shape, 1) % COMP == iota(shape, 0), 1.0 - 2.0 * odd.astype(F32), 0.0)
    table = jnp.concatenate(
        [
            jnp.sum(cross[COMP * r : COMP * r + COMP] * keep, axis=0, keepdims=True)
            for r in range(RECEIVERS)
        ],
        axis=0,
    )
    high = table.astype(BF16)
    low = (table - high.astype(F32)).astype(BF16)
    shape = (SOURCES * COMP, 128)
    group = (iota(shape, 0) // COMP == iota(shape, 1) % 64).astype(F32).astype(BF16)
    table = dot(jnp.concatenate([high, low], axis=0), group)
    table = (table[:RECEIVERS] + table[RECEIVERS:]) * scale
    left = iota((8, 128), 1) < 64
    tab_s[...] = jnp.concatenate(
        [jnp.where(left, table[0:8], table[8:16]), jnp.where(left, table[16:24], table[24:32])], axis=0
    ).astype(BF16)

    pl.semaphore_wait(barrier, 2 * (GROUP - 1))
    send_all("cells", 1, lambda o: tab_s, tab_r)
    send_all("dp", 0, lambda o: data_s.at[o], data_r)

    pick = (
        (iota((128, 128), 0) % 16) * COMP + iota((128, 128), 0) // 16 == iota((128, 128), 1)
    ).astype(F32).astype(BF16)
    for chunk in range(3):
        rows = dot(pick, src_ref[128 * chunk : 128 * chunk + 128, :])
        for c in range(COMP):
            sf[c, 16 * chunk : 16 * chunk + 16, :] = rows[16 * c : 16 * c + 16, :]

    signs = jnp.where(iota((COMP, cells), 0) % 2 == 0, scale, -scale)
    for r in range(RECEIVERS):
        rk[r] = rec_ref[COMP * r : COMP * r + COMP, :].astype(F32) * signs

    def form(r, carry):
        for n in range(cells // 128):
            lanes = slice(128 * n, 128 * n + 128)
            factors = rk[r, :, lanes]
            rows = sf[0, :, lanes] * factors[0:1]
            for c in range(1, COMP):
                rows = rows + sf[c, :, lanes] * factors[c : c + 1]
            ka[r, :, lanes] = rows.astype(BF16)
        return carry

    lax.fori_loop(0, RECEIVERS, form, 0)

    data_r[me_dp] = data_s[me_dp]
    tab_r[me_cells] = tab_s[...]
    wait_all(recv_sem, 0, data_r)
    values, indices = [], []
    for t in range(4):
        tile = beside = data_r[4 * t]
        for sender in range(4 * t + 1, 4 * t + 4):
            here = data_r[sender]
            tile = jnp.where(quarter == lax.rem(me_dp + sender, 4), here, tile)
            beside = jnp.where(quarter == lax.rem(me_dp + sender + 1, 4), here, beside)
        values.append(tile)
        indices.append(pltpu.roll(beside, 96, 1))
    shifted = jnp.concatenate(values, axis=1)
    indices = jnp.concatenate(indices, axis=1)
    column = jnp.transpose(indices)
    code = column[:, 1:2] * SOURCES + column[:, 0:1]
    pairs = RECEIVERS * SOURCES
    oh[...] = (iota((n_data, pairs), 1).astype(F32) == code).astype(F32).astype(BF16)
    source = indices[0:1].astype(jnp.int32)
    receiver = indices[1:2].astype(jnp.int32)
    is_source = (iota((128, n_data), 0) % 64 == source).astype(F32).astype(BF16)
    is_receiver = (iota((32, n_data), 0) == receiver).astype(F32)
    limit = jnp.zeros((REAL, n_data), F32)
    for k in range(REAL):
        limit = jnp.where(row8 == k, huber_ref[k].astype(F32) / 16.0, limit)

    wait_all(recv_sem, 1, tab_r)
    packed = sum_slots(tab_r)
    rows = []
    for t in range(2):
        here = packed[8 * t : 8 * t + 8]
        turned = pltpu.roll(here, 64, 1)
        rows.append(jnp.where(left, here, turned))
        rows.append(jnp.where(left, turned, here))
    spread = dot(split_halves(jnp.concatenate(rows, axis=0)), is_source)
    predicted = jnp.sum(spread * is_receiver, axis=0, keepdims=True)

    def two_parts(x):
        high = x.astype(BF16).astype(F32)
        return jnp.concatenate([high, x - high], axis=0).astype(BF16)

    def weigh(predicted):
        return jnp.clip(predicted - shifted, -limit, limit).astype(BF16)

    def reduce_gradient(phase, whole, part, arrived, meanwhile):
        part[...] = fold(whole).astype(BF16)
        send_all("dp", phase, lambda o: part, arrived)
        arrived[me_dp] = part[...]
        meanwhile()
        wait_all(recv_sem, phase, arrived)
        return unfold(sum_slots(arrived))

    def send_squares(phase, whole, part, arrived):
        squares = jnp.sum(whole * whole, axis=1, keepdims=True)
        diagonal = iota((REAL, 128), 0) == iota((REAL, 128), 1)
        part[...] = jnp.sum(jnp.where(diagonal, squares, 0.0), axis=0, keepdims=True)
        send_all("cells", phase, lambda o: part, arrived)
        arrived[me_cells] = part[...]

    def inverse_scale(arrived):
        total = sum_slots(arrived)
        diagonal = iota((REAL, 128), 0) == iota((REAL, 128), 1)
        column = jnp.sum(jnp.where(diagonal, total, 0.0), axis=1, keepdims=True)
        return 1.0 / jnp.sqrt(column / cells_total + 1e-06)

    def pick_rows():
        kd[...] = dot(oh[...], ka[...].reshape(pairs, cells)).astype(BF16)

    both = dot(two_parts(dot(weigh(predicted), oh[...])), ka[...].reshape(pairs, cells))
    first = reduce_gradient(2, both[:REAL] + both[REAL:], g1_s, g1_r, pick_rows)
    send_squares(4, first, q1_s, q1_r)

    both = dot_nt(two_parts(first), kd[...])
    change = both[:REAL] + both[REAL:]
    dl_s[...] = fold(change).astype(BF16)
    send_all("cells", 3, lambda o: dl_s, dl_r)
    dl_r[me_cells] = dl_s[...]
    wait_all(recv_sem, 4, q1_r)
    inverse1 = inverse_scale(q1_r)
    wait_all(recv_sem, 3, dl_r)
    change = unfold(sum_slots(dl_r))
    whole = dot(weigh(predicted - 0.1 * (change * inverse1)), kd[...])
    second = reduce_gradient(5, whole, g2_s, g2_r, lambda: None)
    send_squares(6, second, q2_s, q2_r)
    velocity = first * inverse1
    base = (start - 0.1 * velocity) - 0.1 * (0.9 * velocity)
    wait_all(recv_sem, 6, q2_r)
    out_ref[...] = base - 0.1 * (second * inverse_scale(q2_r))

    for phase, ref in enumerate((data_r, tab_r, g1_r, dl_r, q1_r, g2_r, q2_r)):
        wait_all(send_sem, phase, ref)


def on_device(source, receiver, source_index, receiver_index, observed, noise, huber, start):
    cells = start.shape[0]
    n_data = source_index.shape[0]
    held = [
        pltpu.VMEM((source.shape[0] * COMP, cells), BF16),
        pltpu.VMEM((receiver.shape[0] * COMP, cells), BF16),
        pltpu.VMEM((1, n_data), jnp.int32),
        pltpu.VMEM((1, n_data), jnp.int32),
        pltpu.VMEM((1, n_data), F32),
        pltpu.VMEM((REAL, n_data), jnp.int32),
        pltpu.SMEM((REAL,), jnp.int32),
        pltpu.VMEM((cells // 128, 128), F32),
    ]

    def pair(shape, dtype):
        return [pltpu.VMEM(shape, dtype), pltpu.VMEM((GROUP,) + shape, dtype)]

    return pl.pallas_call(
        functools.partial(body, cells * GROUP),
        out_shape=pltpu.VMEM((REAL, cells), F32),
        in_specs=[pl.BlockSpec(memory_space=pltpu.HBM)] * 8,
        out_specs=pl.BlockSpec(memory_space=pltpu.VMEM),
        scratch_shapes=held
        + [
            pltpu.VMEM((COMP, SOURCES, cells), F32),
            pltpu.VMEM((RECEIVERS, COMP, cells), F32),
            pltpu.VMEM((RECEIVERS, SOURCES, cells), BF16),
            pltpu.VMEM((n_data, cells), BF16),
            pltpu.VMEM((n_data, RECEIVERS * SOURCES), BF16),
            pltpu.VMEM((GROUP, 8, 128), F32),
            pltpu.VMEM((GROUP, 8, 128), F32),
        ]
        + pair((16, 128), BF16)
        + pair((16, cells // 2), BF16)
        + pair((16, n_data // 2), BF16)
        + pair((1, 128), F32)
        + pair((16, cells // 2), BF16)
        + pair((1, 128), F32)
        + [
            pltpu.SemaphoreType.DMA((7,)),
            pltpu.SemaphoreType.DMA((7,)),
            pltpu.SemaphoreType.DMA((8,)),
        ],
        compiler_params=pltpu.CompilerParams(collective_id=0, has_side_effects=True),
    )(
        source.reshape(-1, cells),
        receiver.reshape(-1, cells),
        source_index.reshape(1, n_data),
        receiver_index.reshape(1, n_data),
        observed.reshape(1, n_data),
        noise,
        huber,
        start.reshape(-1, 128),
    )


def solution(mesh):
    placed = (
        P(None, None, "cells"),
        P("dp", None, "cells"),
        P("dp"),
        P("dp"),
        P("dp"),
        P(None, "dp"),
        P(),
        P("cells"),
    )
    return jax.shard_map(
        on_device, mesh=mesh, in_specs=placed, out_specs=P(None, "cells"), check_vma=False
    )
```

```python
import functools
import math

import jax
import jax.numpy as jnp
from jax import lax
from jax.experimental import pallas as pl
from jax.experimental.pallas import tpu as pltpu
from jax.sharding import PartitionSpec as P

F32 = jnp.float32
BF16 = jnp.bfloat16
GROUP = 16
COMP = 8
REAL = 8
SOURCES = 48
RECEIVERS = 32
LOGICAL = pl.DeviceIdType.LOGICAL


def hops(step, ring):
    return min(step, ring - step)


CELLS_ORDER = sorted(
    ((step, flip) for step in range(8) for flip in range(2) if step or flip),
    key=lambda p: -(hops(p[0], 8) + 2 * p[1]),
)
DP_ORDER = sorted(
    ((y, x, core) for y in range(4) for x in range(2) for core in range(2) if y or x or core),
    key=lambda p: -((0, 1, 2, 1)[p[0]] + p[1] + 0.1 * p[2]),
)


def iota(shape, axis):
    return lax.broadcasted_iota(jnp.int32, shape, axis)


def dot(a, b):
    return jnp.dot(a, b, preferred_element_type=F32)


def dot_nt(a, b):
    return lax.dot_general(a, b, (((1,), (1,)), ((), ())), preferred_element_type=F32)


def split_halves(table):
    high = table.astype(BF16).astype(F32)
    return jnp.where(iota(table.shape, 1) < 64, high, table - high).astype(BF16)


def body(
    cells_total,
    *refs,
):
    given, (base_ref, step_ref), held, refs = refs[:8], refs[8:10], refs[10:18], refs[18:]
    src_ref, rec_ref, sidx_ref, ridx_ref, obs_ref, noise_ref, huber_ref, start_ref = held
    sf, rk, ka, kd, oh, data_s, data_r, tab_s, tab_r, g1_s, g1_r, dl_s, dl_r, q1_s, q1_r = refs[:15]
    g2_s, g2_r, q2_s, q2_r, send_sem, recv_sem, load_sem = refs[15:]
    me_dp = lax.axis_index("dp")
    me_cells = lax.axis_index("cells")
    cells = src_ref.shape[1]
    n_data = sidx_ref.shape[1]
    scale = 0.2 / math.sqrt(COMP * cells_total)

    def flipped(value, bit, flip):
        return lax.rem(value // bit + flip, 2) * bit

    def peer(axis, pattern):
        if axis == "cells":
            step, flip = pattern
            return 2 * lax.rem(me_cells // 2 + step, 8) + flipped(me_cells, 1, flip)
        y, x, core = pattern
        me = me_dp
        return (
            flipped(me, 8, y // 2) + flipped(me, 4, y % 2) + flipped(me, 2, x) + flipped(me, 1, core)
        )

    peers = {
        "cells": [(peer("cells", p), me_dp * GROUP + peer("cells", p)) for p in CELLS_ORDER],
        "dp": [(peer("dp", p), peer("dp", p) * GROUP + me_cells) for p in DP_ORDER],
    }

    barrier = pltpu.get_barrier_semaphore()

    def greet(axis, patterns):
        for _, device in patterns:
            pl.semaphore_signal(barrier, inc=1, device_id=device, device_id_type=LOGICAL)

    greet("cells", peers["cells"][:8])
    loads = [
        pltpu.make_async_copy(a, b, load_sem.at[n]) for n, (a, b) in enumerate(zip(given, held))
    ]
    for n in (3, 2, 4, 5, 1, 7, 0, 6):
        loads[n].start()
    greet("cells", peers["cells"][8:])
    greet("dp", peers["dp"])

    def send_all(axis, phase, src_of, arrived):
        mine = me_cells if axis == "cells" else me_dp
        for other, device in peers[axis]:
            pltpu.make_async_remote_copy(
                src_ref=src_of(other),
                dst_ref=arrived.at[mine],
                send_sem=send_sem.at[phase],
                recv_sem=recv_sem.at[phase],
                device_id=device,
                device_id_type=LOGICAL,
            ).start()

    def fold(x):
        half = x.shape[1] // 2
        return jnp.concatenate([x[:, :half], x[:, half:]], axis=0)

    def unfold(x):
        half = x.shape[0] // 2
        return jnp.concatenate([x[:half], x[half:]], axis=1)

    def sum_slots(arrived):
        parts = [arrived[o].astype(F32) for o in range(GROUP)]
        while len(parts) > 1:
            parts = [a + b for a, b in zip(parts[::2], parts[1::2])]
        return parts[0]

    def wait_all(sem, phase, ref):
        part = ref.at[pl.ds(0, GROUP - 1)]
        pltpu.make_async_copy(part, part, sem.at[phase]).wait()

    for n in range(2, 7):
        loads[n].wait()
    owner = ridx_ref[...] // 32
    local = ridx_ref[...] % 32
    member = (iota((16, n_data), 0) == owner).astype(F32)
    before = (iota((n_data, n_data), 0) < iota((n_data, n_data), 1)).astype(F32).astype(BF16)
    rank = jnp.sum(member * dot(member.astype(BF16), before), axis=0, keepdims=True)
    place = (128 * (owner // 4) + 32 * ((owner + me_dp) % 4)).astype(F32) + rank
    move = (iota((n_data, n_data), 0).astype(F32) == place).astype(F32).astype(BF16)
    shifted = obs_ref[...] + noise_ref[...].astype(F32) / 4096.0
    high = shifted.astype(BF16).astype(F32)
    middle = (shifted - high).astype(BF16).astype(F32)
    low = shifted - high - middle
    row8 = iota((8, n_data), 0)
    index_rows = jnp.where(
        row8 == 0,
        sidx_ref[...].astype(F32),
        jnp.where(row8 == 1, local.astype(F32), 0.0),
    )
    moved = dot_nt(jnp.concatenate([high, middle, low, index_rows], axis=0).astype(BF16), move)
    shifted = moved[0:8] + moved[8:16] + moved[16:24]
    quarter = iota((8, 128), 1) // 32
    for t in range(4):
        lanes = slice(128 * t, 128 * t + 128)
        beside = pltpu.roll(moved[24:32, lanes], 32, 1)
        for o in range(4 * t, 4 * t + 4):
            data_s[o] = jnp.where(quarter == lax.rem(me_dp + o, 4), shifted[:, lanes], beside)

    for n in (1, 7):
        loads[n].wait()
    start = jnp.concatenate([start_ref[n : n + 1, :] for n in range(cells // 128)], axis=1)
    exact = rec_ref[...].astype(F32) * start.astype(BF16).astype(F32)
    high = exact.astype(BF16)
    low = (exact - high.astype(F32)).astype(BF16)
    loads[0].wait()
    cross = dot_nt(high, src_ref[...]) + dot_nt(low, src_ref[...])
    shape = (COMP, SOURCES * COMP)
    odd = iota(shape, 0) % 2
    keep = jnp.where(iota(shape, 1) % COMP == iota(shape, 0), 1.0 - 2.0 * odd.astype(F32), 0.0)
    table = jnp.concatenate(
        [
            jnp.sum(cross[COMP * r : COMP * r + COMP] * keep, axis=0, keepdims=True)
            for r in range(RECEIVERS)
        ],
        axis=0,
    )
    high = table.astype(BF16)
    low = (table - high.astype(F32)).astype(BF16)
    shape = (SOURCES * COMP, 128)
    group = (iota(shape, 0) // COMP == iota(shape, 1) % 64).astype(F32).astype(BF16)
    table = dot(jnp.concatenate([high, low], axis=0), group)
    table = (table[:RECEIVERS] + table[RECEIVERS:]) * scale
    left = iota((8, 128), 1) < 64
    tab_s[...] = jnp.concatenate(
        [jnp.where(left, table[0:8], table[8:16]), jnp.where(left, table[16:24], table[24:32])], axis=0
    ).astype(BF16)

    pl.semaphore_wait(barrier, 2 * (GROUP - 1))
    send_all("cells", 1, lambda o: tab_s, tab_r)
    send_all("dp", 0, lambda o: data_s.at[o], data_r)

    pick = (
        (iota((128, 128), 0) % 16) * COMP + iota((128, 128), 0) // 16 == iota((128, 128), 1)
    ).astype(F32).astype(BF16)
    for chunk in range(3):
        rows = dot(pick, src_ref[128 * chunk : 128 * chunk + 128, :])
        for c in range(COMP):
            sf[c, 16 * chunk : 16 * chunk + 16, :] = rows[16 * c : 16 * c + 16, :]

    signs = jnp.where(iota((COMP, cells), 0) % 2 == 0, scale, -scale)
    for r in range(RECEIVERS):
        rk[r] = rec_ref[COMP * r : COMP * r + COMP, :].astype(F32) * signs

    def form(r, carry):
        for n in range(cells // 128):
            lanes = slice(128 * n, 128 * n + 128)
            factors = rk[r, :, lanes]
            rows = sf[0, :, lanes] * factors[0:1]
            for c in range(1, COMP):
                rows = rows + sf[c, :, lanes] * factors[c : c + 1]
            ka[r, :, lanes] = rows.astype(BF16)
        return carry

    lax.fori_loop(0, RECEIVERS, form, 0)

    data_r[me_dp] = data_s[me_dp]
    tab_r[me_cells] = tab_s[...]
    wait_all(recv_sem, 0, data_r)
    values, indices = [], []
    for t in range(4):
        tile = beside = data_r[4 * t]
        for sender in range(4 * t + 1, 4 * t + 4):
            here = data_r[sender]
            tile = jnp.where(quarter == lax.rem(me_dp + sender, 4), here, tile)
            beside = jnp.where(quarter == lax.rem(me_dp + sender + 1, 4), here, beside)
        values.append(tile)
        indices.append(pltpu.roll(beside, 96, 1))
    shifted = jnp.concatenate(values, axis=1)
    indices = jnp.concatenate(indices, axis=1)
    column = jnp.transpose(indices)
    code = column[:, 1:2] * SOURCES + column[:, 0:1]
    pairs = RECEIVERS * SOURCES
    oh[...] = (iota((n_data, pairs), 1).astype(F32) == code).astype(F32).astype(BF16)
    source = indices[0:1].astype(jnp.int32)
    receiver = indices[1:2].astype(jnp.int32)
    is_source = (iota((128, n_data), 0) % 64 == source).astype(F32).astype(BF16)
    is_receiver = (iota((32, n_data), 0) == receiver).astype(F32)
    limit = jnp.zeros((REAL, n_data), F32)
    for k in range(REAL):
        limit = jnp.where(row8 == k, huber_ref[k].astype(F32) / 16.0, limit)

    wait_all(recv_sem, 1, tab_r)
    packed = sum_slots(tab_r)
    rows = []
    for t in range(2):
        here = packed[8 * t : 8 * t + 8]
        turned = pltpu.roll(here, 64, 1)
        rows.append(jnp.where(left, here, turned))
        rows.append(jnp.where(left, turned, here))
    spread = dot(split_halves(jnp.concatenate(rows, axis=0)), is_source)
    predicted = jnp.sum(spread * is_receiver, axis=0, keepdims=True)

    def two_parts(x):
        high = x.astype(BF16).astype(F32)
        return jnp.concatenate([high, x - high], axis=0).astype(BF16)

    def weigh(predicted):
        return jnp.clip(predicted - shifted, -limit, limit).astype(BF16)

    def reduce_gradient(phase, whole, part, arrived, meanwhile):
        part[...] = fold(whole).astype(BF16)
        send_all("dp", phase, lambda o: part, arrived)
        arrived[me_dp] = part[...]
        meanwhile()
        wait_all(recv_sem, phase, arrived)
        return unfold(sum_slots(arrived))

    def send_squares(phase, whole, part, arrived):
        squares = jnp.sum(whole * whole, axis=1, keepdims=True)
        diagonal = iota((REAL, 128), 0) == iota((REAL, 128), 1)
        part[...] = jnp.sum(jnp.where(diagonal, squares, 0.0), axis=0, keepdims=True)
        send_all("cells", phase, lambda o: part, arrived)
        arrived[me_cells] = part[...]

    def inverse_scale(arrived):
        total = sum_slots(arrived)
        diagonal = iota((REAL, 128), 0) == iota((REAL, 128), 1)
        column = jnp.sum(jnp.where(diagonal, total, 0.0), axis=1, keepdims=True)
        return 1.0 / jnp.sqrt(column / cells_total + 1e-06)

    def pick_rows():
        kd[...] = dot(oh[...], ka[...].reshape(pairs, cells)).astype(BF16)

    both = dot(two_parts(dot(weigh(predicted), oh[...])), ka[...].reshape(pairs, cells))
    first = reduce_gradient(2, both[:REAL] + both[REAL:], g1_s, g1_r, pick_rows)
    send_squares(4, first, q1_s, q1_r)

    both = dot_nt(two_parts(first), kd[...])
    change = both[:REAL] + both[REAL:]
    dl_s[...] = fold(change).astype(BF16)
    send_all("cells", 3, lambda o: dl_s, dl_r)
    dl_r[me_cells] = dl_s[...]
    wait_all(recv_sem, 4, q1_r)
    inverse1 = inverse_scale(q1_r)
    wait_all(recv_sem, 3, dl_r)
    change = unfold(sum_slots(dl_r))
    whole = dot(weigh(predicted - 0.1 * (change * inverse1)), kd[...])
    second = reduce_gradient(5, whole, g2_s, g2_r, lambda: None)
    send_squares(6, second, q2_s, q2_r)
    velocity = first * inverse1
    base_ref[...] = (start - 0.1 * velocity) - 0.1 * (0.9 * velocity)
    wait_all(recv_sem, 6, q2_r)
    step_ref[...] = 0.1 * (second * inverse_scale(q2_r))

    for phase, ref in enumerate((data_r, tab_r, g1_r, dl_r, q1_r, g2_r, q2_r)):
        wait_all(send_sem, phase, ref)


def on_device(source, receiver, source_index, receiver_index, observed, noise, huber, start):
    cells = start.shape[0]
    n_data = source_index.shape[0]
    held = [
        pltpu.VMEM((source.shape[0] * COMP, cells), BF16),
        pltpu.VMEM((receiver.shape[0] * COMP, cells), BF16),
        pltpu.VMEM((1, n_data), jnp.int32),
        pltpu.VMEM((1, n_data), jnp.int32),
        pltpu.VMEM((1, n_data), F32),
        pltpu.VMEM((REAL, n_data), jnp.int32),
        pltpu.SMEM((REAL,), jnp.int32),
        pltpu.VMEM((cells // 128, 128), F32),
    ]

    def pair(shape, dtype):
        return [pltpu.VMEM(shape, dtype), pltpu.VMEM((GROUP,) + shape, dtype)]

    base, step = pl.pallas_call(
        functools.partial(body, cells * GROUP),
        out_shape=[pltpu.VMEM((REAL, cells), F32)] * 2,
        in_specs=[pl.BlockSpec(memory_space=pltpu.HBM)] * 8,
        out_specs=[pl.BlockSpec(memory_space=pltpu.VMEM)] * 2,
        scratch_shapes=held
        + [
            pltpu.VMEM((COMP, SOURCES, cells), F32),
            pltpu.VMEM((RECEIVERS, COMP, cells), F32),
            pltpu.VMEM((RECEIVERS, SOURCES, cells), BF16),
            pltpu.VMEM((n_data, cells), BF16),
            pltpu.VMEM((n_data, RECEIVERS * SOURCES), BF16),
            pltpu.VMEM((GROUP, 8, 128), F32),
            pltpu.VMEM((GROUP, 8, 128), F32),
        ]
        + pair((16, 128), BF16)
        + pair((16, cells // 2), BF16)
        + pair((16, n_data // 2), BF16)
        + pair((1, 128), F32)
        + pair((16, cells // 2), BF16)
        + pair((1, 128), F32)
        + [
            pltpu.SemaphoreType.DMA((7,)),
            pltpu.SemaphoreType.DMA((7,)),
            pltpu.SemaphoreType.DMA((8,)),
        ],
        compiler_params=pltpu.CompilerParams(collective_id=0, has_side_effects=True),
    )(
        source.reshape(-1, cells),
        receiver.reshape(-1, cells),
        source_index.reshape(1, n_data),
        receiver_index.reshape(1, n_data),
        observed.reshape(1, n_data),
        noise,
        huber,
        start.reshape(-1, 128),
    )
    return base - step


def solution(mesh):
    placed = (
        P(None, None, "cells"),
        P("dp", None, "cells"),
        P("dp"),
        P("dp"),
        P("dp"),
        P(None, "dp"),
        P(),
        P("cells"),
    )
    return jax.shard_map(
        on_device, mesh=mesh, in_specs=placed, out_specs=P(None, "cells"), check_vma=False
    )
```
